32 devices in a mesh: prow: 8 (over z, core), pcol: 4 (over y, x).
Axes of the slice: x: 2, y: 2, z: 4, core: 2. Of those that a mesh axis runs over, the one named last changes fastest.
Arguments:
- right_side: float32 [1024, 4, 4, 1024], P('prow', None, 'pcol'), may hold values from -6 to 6
- inverse_blocks: bfloat16 [2, 1, 8, 1024, 2, 4, 1024], P(None, None, 'prow', None, None, 'pcol'), as said below
- coupling: bfloat16 [1, 8, 1024, 2, 4, 1024], P(None, 'prow', None, None, 'pcol'), may hold values from -0.03125 to 0.03125
- pivots: int32 [2, 8, 1024], P(None, 'prow'), may hold values from 0 to 16383, as said below
Outputs:
- solution: bfloat16 [1024, 2, 8, 1024], P('pcol', None, 'prow')
The draws below stay inside these ranges and needn't reach their ends.
Inputs may be any that keep to these rules, and one draw needn't show every extreme that they name: `inverse_blocks`: each block is unit upper triangular: ones on its diagonal, zeros below it. Every row number of the window appears exactly once; for every p and p2, exactly 16 * 1024 / 8 ** 2 of the entries pivots[:, p, :] are rows g with (g // 1024) % 8 == p2.
All inputs are finite; a program needn't handle non-finite values.
Results may differ from the reference program's by a relative error of at most 0.0052.
Values may be sent and summed in bfloat16 or wider, within the bound.
A program may use at most 128 MiB of HBM per device.

```python
import math
import jax
import jax.numpy as jnp
from jax import lax

NB = 1024
NRHS = 1024
SB = 8
WT = 16
N_PROW = 8
N_PCOL = 4


def draw_inverse_blocks(key, part):
    block_span = SB * NB
    row_ids = lax.broadcasted_iota(jnp.int32, (block_span, block_span), 0)
    col_ids = lax.broadcasted_iota(jnp.int32, (block_span, block_span), 1)
    upper_mask = (col_ids > row_ids).astype(jnp.float32)
    diagonal = (col_ids == row_ids).astype(jnp.float32)
    keys = jax.random.split(key, 4)

    def one_block(noise_key, scale_key):
        noise = jax.random.normal(noise_key, (block_span, block_span), jnp.float32)
        return diagonal + upper_mask * noise * (0.7 / math.sqrt(block_span))
    blocks = jnp.stack([one_block(keys[0], keys[1]), one_block(keys[2], keys[3])])
    return blocks.reshape(2, SB // N_PROW, N_PROW, NB, SB // N_PCOL, N_PCOL, NB).astype(jnp.bfloat16)


def draw_pivots(key, part):
    local_rows = WT // N_PROW * NB
    share = local_rows // N_PROW
    source_keys = jax.random.split(jax.random.fold_in(key, 11), N_PROW)
    target_keys = jax.random.split(jax.random.fold_in(key, 23), N_PROW)
    source_local = jax.vmap(lambda k: jax.random.permutation(k, local_rows))(source_keys).astype(jnp.int32)
    source_ids = lax.broadcasted_iota(jnp.int32, (N_PROW, local_rows), 0)
    global_rows = (source_local // NB * N_PROW + source_ids) * NB + source_local % NB
    grouped = global_rows.reshape(N_PROW, N_PROW, share).transpose(1, 0, 2).reshape(N_PROW, local_rows)
    shuffle = jax.vmap(lambda k: jax.random.permutation(k, local_rows))(target_keys).astype(jnp.int32)
    target_lists = jnp.take_along_axis(grouped, shuffle, axis=1)
    return target_lists.reshape(N_PROW, WT // N_PROW, NB).transpose(1, 0, 2).astype(jnp.int32)


def steps_of(own_key, shape, shards, smallest, largest):
    level, own = 1.0, jax.random.fold_in(own_key, 6)
    for dim, parts in shards:
        draws = jnp.exp(jax.random.uniform(jax.random.fold_in(own, dim), (parts,), jnp.float32, smallest / len(shards), largest / len(shards)))
        level = level * jnp.repeat(draws, shape[dim] // parts).reshape([-1 if axis == dim else 1 for axis in range(len(shape))])
    return level


def bell_draw(rng, shape, deviation, limit, cuts=(), kind=jnp.bfloat16):
    result = jax.random.normal(rng, shape, jnp.float32) * deviation
    if len(cuts) > 0:
        result = steps_of(rng, shape, cuts, -0.22, 0.18) * result
    return jnp.clip(result, min=-limit, max=limit).astype(kind)


def setup_inputs(seed: int = 0) -> dict:
    key_of = jax.random.split(jax.random.key(seed), 5)
    return {
        "right_side": bell_draw(key_of[0], (NRHS, WT // N_PCOL, N_PCOL, NB), 1.0, 6.0, ((0, 8), (2, 4)), jnp.float32),
        "inverse_blocks": draw_inverse_blocks(jax.random.fold_in(key_of[4], 71), 0),
        "coupling": bell_draw(key_of[2], (SB // N_PROW, N_PROW, NB, SB // N_PCOL, N_PCOL, NB), (4 * SB * NB) ** -0.5, 0.03125, ((1, 8), (4, 4))),
        "pivots": draw_pivots(jax.random.fold_in(key_of[4], 71), 0),
    }


def reference(right_side, inverse_blocks, coupling, pivots):
    block_span = SB * NB
    window_rhs = right_side.reshape(NRHS, WT * NB)
    inverse_pair = inverse_blocks.reshape(2, block_span, block_span)
    coupling_mat = coupling.reshape(block_span, block_span)
    contract_last = (((1,), (1,)), ((), ()))
    upper_ready = window_rhs[:, block_span:].astype(jnp.bfloat16)
    upper_solved = lax.dot_general(upper_ready, inverse_pair[1], contract_last, preferred_element_type=jnp.float32).astype(jnp.bfloat16)
    update = jnp.dot(upper_solved, coupling_mat, preferred_element_type=jnp.float32)
    lower_ready = (window_rhs[:, :block_span] - update).astype(jnp.bfloat16)
    lower_solved = lax.dot_general(lower_ready, inverse_pair[0], contract_last, preferred_element_type=jnp.float32).astype(jnp.bfloat16)
    joined = jnp.concatenate([lower_solved, upper_solved], axis=1)
    permuted = jnp.take(joined, pivots.reshape(WT * NB).astype(jnp.int32), axis=1)
    return permuted.reshape(NRHS, WT // N_PROW, N_PROW, NB)
```

```python
import functools

import jax
import jax.numpy as jnp
from jax import lax
from jax.experimental import pallas as pl
from jax.experimental.pallas import tpu as pltpu
from jax.sharding import PartitionSpec as P

BF16 = jnp.bfloat16
F32 = jnp.float32
MESH = pl.DeviceIdType.MESH
PARTS = 2
CORES = 2
NT = (((1,), (1,)), ((), ()))
NN = (((1,), (0,)), ((), ()))


def tile_of(size):
    return 256 if size % 256 == 0 else 128


def span(index, size):
    return pl.ds(pl.multiple_of(index * size, size), size)


def meet(sizes):
    barrier = pltpu.get_barrier_semaphore()
    count = 0
    for name, size in sizes:
        place = lax.axis_index(name)
        for step in range(1, size):
            peer = lax.rem(place + step, size)
            pl.semaphore_signal(barrier, inc=1, device_id={name: peer}, device_id_type=MESH)
            count += 1
    pl.semaphore_wait(barrier, count)


def spread_order(size):
    half = size // 2
    return sorted(range(1, size), key=lambda step: (step == half, step))


def start_sums(lhs_ref, mat_ref, own_ref, send_ref, recv_ref, send_sem, recv_sem, size):
    place = lax.axis_index("pcol")
    own, width = own_ref.shape
    tile = tile_of(width)
    part = own // PARTS
    each = own // lhs_ref.shape[1]

    def product(target, store):
        sources = pl.ds(target * each, each)

        @pl.loop(0, width // tile)
        def _(step):
            cols = span(step, tile)
            store(
                cols,
                lax.dot_general(
                    lhs_ref[sources].reshape(own, lhs_ref.shape[2]),
                    mat_ref[cols, :],
                    NT,
                    preferred_element_type=F32,
                ),
            )

    def copy_of(piece, step):
        rows = pl.ds(piece * part, part)
        return pltpu.make_async_remote_copy(
            src_ref=send_ref.at[step - 1, rows],
            dst_ref=recv_ref.at[step - 1, rows],
            send_sem=send_sem.at[piece, step - 1],
            recv_sem=recv_sem.at[piece, step - 1],
            device_id={"pcol": lax.rem(place + step, size)},
            device_id_type=MESH,
        )

    copies = {}
    for step in spread_order(size):

        def keep(cols, value, step=step):
            send_ref[step - 1, :, cols] = value.astype(BF16)

        product(lax.rem(place + step, size), keep)
        copies[0, step] = copy_of(0, step)
        copies[0, step].start()
    for piece in range(1, PARTS):
        for step in spread_order(size):
            copies[piece, step] = copy_of(piece, step)
            copies[piece, step].start()

    def hold(cols, value):
        own_ref[:, cols] = value

    product(place, hold)
    return copies


def finish_sum(copies, piece, own_ref, recv_ref, size):
    own = own_ref.shape[0]
    part = own // PARTS
    rows = pl.ds(piece * part, part)
    for step in spread_order(size):
        copies[piece, step].wait_recv()
    total = own_ref[rows, :]
    for step in range(1, size):
        total = total + recv_ref[step - 1, rows, :].astype(F32)
    return total.astype(BF16)


def upper_kernel(
    size, line, rhs_ref, inv_ref, coup_ref, upd_ref, solved_ref,
    all_ref, prod_ref, own_ref, send_ref, recv_ref, full_ref,
    rsend_sem, rrecv_sem, psend_sem, precv_sem, send_sem, recv_sem, gsend_sem, grecv_sem,
):
    chips = line // CORES
    here = lax.axis_index("prow")
    place = lax.axis_index("pcol")
    chip = here // CORES
    core = lax.rem(here, CORES)
    right = lax.rem(chip + 1, chips) * CORES + core
    left = lax.rem(chip + chips - 1, chips) * CORES + core
    partner = chip * CORES + (CORES - 1 - core)
    peers = [lax.rem(place + step, size) for step in range(1, size)]

    barrier = pltpu.get_barrier_semaphore()
    for device in (right, left, partner):
        pl.semaphore_signal(barrier, inc=1, device_id={"prow": device}, device_id_type=MESH)
    for device in peers:
        pl.semaphore_signal(barrier, inc=1, device_id={"pcol": device}, device_id_type=MESH)
    pl.semaphore_wait(barrier, 3 + len(peers))

    rhs_here, depth = rhs_ref.shape
    rows = CORES * rhs_here
    part = rows // size
    width = inv_ref.shape[0]
    count = coup_ref.shape[1]
    tile = tile_of(width)
    wide = tile_of(count)

    def remote(src, dst, sends, recvs, axis, device):
        return pltpu.make_async_remote_copy(
            src_ref=src, dst_ref=dst, send_sem=sends, recv_sem=recvs,
            device_id={axis: device}, device_id_type=MESH,
        )

    ring, pairs, sums, shares = {}, {}, {}, {}

    def chip_of(stage):
        return lax.rem(chip + chips - stage, chips)

    def collect(stage):
        slot = chip_of(stage) * CORES + core
        source = rhs_ref if stage == 0 else all_ref.at[slot]
        if stage > 0:
            ring[stage - 1].wait_recv()
        if stage < chips - 1:
            ring[stage] = remote(
                source, all_ref.at[slot], rsend_sem.at[stage], rrecv_sem.at[stage], "prow", right
            )
            ring[stage].start()
        pairs[stage] = remote(
            source, all_ref.at[slot], psend_sem.at[stage], precv_sem.at[stage], "prow", partner
        )
        pairs[stage].start()
        if stage == 0:
            all_ref[slot] = rhs_ref[...]
        pairs[stage].wait_recv()

    def multiply(stage):
        first = chip_of(stage) * CORES

        @pl.loop(0, width // tile)
        def _(step):
            cols = span(step, tile)
            lhs = all_ref[pl.ds(first, CORES)].reshape(rows, depth)
            value = lax.dot_general(lhs, inv_ref[cols, :], NT, preferred_element_type=F32)
            for owner in range(size):
                piece = value[owner * part : (owner + 1) * part]
                prod_ref[owner, :, cols] = piece
                send_ref[stage, owner, :, cols] = piece.astype(BF16)

        own_ref[stage] = prod_ref[place]
        for index, peer in enumerate(peers):
            sums[stage, index] = remote(
                send_ref.at[stage, peer], recv_ref.at[stage, index],
                send_sem.at[stage, index], recv_sem.at[stage, index], "pcol", peer,
            )
            sums[stage, index].start()

    def settle(stage):
        total = own_ref[stage]
        for index in range(size - 1):
            sums[stage, index].wait_recv()
            total = total + recv_ref[stage, index].astype(F32)
        full_ref[stage, place] = total.astype(BF16)
        for index, peer in enumerate(peers):
            shares[stage, index] = remote(
                full_ref.at[stage, place], full_ref.at[stage, place],
                gsend_sem.at[stage, index], grecv_sem.at[stage, index], "pcol", peer,
            )
            shares[stage, index].start()

    def couple(stage):
        for index in range(size - 1):
            shares[stage, index].wait_recv()
        target = span(chip_of(stage), rows)
        solved_ref[target, :] = full_ref[stage].reshape(rows, width)

        @pl.loop(0, count // wide)
        def _(step):
            cols = span(step, wide)
            upd_ref[target, cols] = lax.dot_general(
                solved_ref[target, :], coup_ref[:, cols], NN, preferred_element_type=F32
            ).astype(BF16)

    for stage in range(chips + 2):
        if stage < chips:
            collect(stage)
            multiply(stage)
        if 1 <= stage <= chips:
            settle(stage - 1)
        if stage >= 2:
            couple(stage - 2)
    for group in (ring, pairs, sums, shares):
        for copy in group.values():
            copy.wait_send()


def lower_kernel(
    size, line, rhs_ref, inv_ref, upper_ref, picked_ref, code_ref, out_ref,
    own_ref, send_ref, recv_ref, pass_ref, take_ref, all_ref,
    rsend_sem, rrecv_sem, psend_sem, precv_sem, send_sem, recv_sem, xsend_sem, xrecv_sem,
):
    meet((("pcol", size), ("prow", line)))
    place = lax.axis_index("prow")
    own, width = own_ref.shape
    part = own // PARTS
    share = picked_ref.shape[2]
    count = out_ref.shape[1]
    tile = tile_of(count)
    chips = line // CORES
    chip = place // CORES
    core = lax.rem(place, CORES)
    right = lax.rem(chip + 1, chips) * CORES + core
    partner = chip * CORES + (CORES - 1 - core)
    ring, pairs = [], []
    for stage in range(chips):
        slot = lax.rem(chip + chips - stage, chips) * CORES + core
        source = rhs_ref if stage == 0 else all_ref.at[slot]
        if stage > 0:
            ring[stage - 1].wait_recv()
        if stage < chips - 1:
            ring.append(
                pltpu.make_async_remote_copy(
                    src_ref=source, dst_ref=all_ref.at[slot],
                    send_sem=rsend_sem.at[stage], recv_sem=rrecv_sem.at[stage],
                    device_id={"prow": right}, device_id_type=MESH,
                )
            )
            ring[stage].start()
        pairs.append(
            pltpu.make_async_remote_copy(
                src_ref=source, dst_ref=all_ref.at[slot],
                send_sem=psend_sem.at[stage], recv_sem=precv_sem.at[stage],
                device_id={"prow": partner}, device_id_type=MESH,
            )
        )
        pairs[stage].start()
        if stage == 0:
            all_ref[slot] = rhs_ref[...]
    for copy in pairs:
        copy.wait_recv()
    copies = start_sums(
        all_ref, inv_ref, own_ref, send_ref, recv_ref, send_sem, recv_sem, size
    )
    row_ids = lax.broadcasted_iota(jnp.int32, (width, share), 0)
    moves = []
    for piece in range(PARTS):
        rows = pl.ds(piece * part, part)
        lower = finish_sum(copies, piece, own_ref, recv_ref, size)
        upper = upper_ref[rows, :]
        for step in list(range(1, line)) + [0]:
            target = lax.rem(place + step, line)
            wanted = picked_ref[target]
            low = jnp.where(row_ids == wanted, 1.0, 0.0).astype(BF16)
            high = jnp.where(row_ids + width == wanted, 1.0, 0.0).astype(BF16)
            chosen = (
                lax.dot_general(lower, low, NN, preferred_element_type=F32)
                + lax.dot_general(upper, high, NN, preferred_element_type=F32)
            ).astype(BF16)
            if step == 0:
                take_ref[0, rows, :] = chosen
                continue
            pass_ref[step - 1, rows, :] = chosen
            move = pltpu.make_async_remote_copy(
                src_ref=pass_ref.at[step - 1, rows],
                dst_ref=take_ref.at[step, rows],
                send_sem=xsend_sem.at[piece, step - 1],
                recv_sem=xrecv_sem.at[piece, step - 1],
                device_id={"prow": target},
                device_id_type=MESH,
            )
            move.start()
            moves.append(move)
    for move in moves:
        move.wait_recv()
    slot_ids = lax.broadcasted_iota(jnp.int32, (share, tile), 0)

    @pl.loop(0, count // tile)
    def _(step):
        cols = span(step, tile)
        code = code_ref[:, cols]
        total = jnp.zeros((own, tile), F32)
        for source in range(line):
            spot = jnp.where(slot_ids + source * share == code, 1.0, 0.0).astype(BF16)
            total = total + lax.dot_general(
                take_ref[source], spot, NN, preferred_element_type=F32
            )
        out_ref[:, cols] = total.astype(BF16)

    for copy in ring + pairs + list(copies.values()) + moves:
        copy.wait_send()


def params(number):
    return pltpu.CompilerParams(
        collective_id=number, has_side_effects=True, vmem_limit_bytes=60 * 1024 * 1024
    )


def in_vmem(count):
    return [pl.BlockSpec(memory_space=pltpu.VMEM)] * count


def sum_scratch(size, own, width):
    return [
        pltpu.VMEM((own, width), F32),
        pltpu.VMEM((size - 1, own, width), BF16),
        pltpu.VMEM((size - 1, own, width), BF16),
    ]


def dma(*shape):
    return pltpu.SemaphoreType.DMA(shape)


def body(right_side, inverse_blocks, coupling, pivots):
    rhs_here = right_side.shape[0]
    tile_width = right_side.shape[3]
    blocks_here = inverse_blocks.shape[1]
    count_rows = blocks_here * tile_width
    tiles_half = inverse_blocks.shape[4]
    count_cols = tiles_half * tile_width
    inverse_pair = inverse_blocks.reshape(2, count_rows, count_cols)
    coupling_mat = coupling.reshape(count_rows, count_cols)
    line = lax.axis_size("prow")
    size = lax.axis_size("pcol")
    rhs_total = rhs_here * line
    own = rhs_total // size
    me = lax.axis_index("prow")

    lower_rhs = right_side[:, :tiles_half].reshape(rhs_here, count_cols)
    upper_rhs = right_side[:, tiles_half:].astype(BF16).reshape(rhs_here, count_cols)

    own_pivots = pivots.reshape(-1)
    width = own_pivots.shape[0]
    share = width // line
    all_pivots = lax.all_gather(own_pivots, "prow", axis=0)

    def owner_of(rows):
        return rows // tile_width % line

    def local_of(rows):
        return rows // (tile_width * line) * tile_width + rows % tile_width

    def ranks(marks):
        before = lax.broadcasted_iota(jnp.int32, (width, width), 0)
        after = lax.broadcasted_iota(jnp.int32, (width, width), 1)
        counts = jnp.dot(
            marks.astype(BF16), (before < after).astype(BF16), preferred_element_type=F32
        )
        return counts.astype(jnp.int32)

    mine = owner_of(all_pivots) == me
    owner = owner_of(own_pivots)
    same = owner[None, :] == lax.broadcasted_iota(jnp.int32, (line, 1), 0)
    counted = ranks(jnp.concatenate([mine, same], axis=0))
    slot = jnp.where(mine, counted[:line], -1)
    hits = slot[:, :, None] == lax.broadcasted_iota(jnp.int32, (1, 1, share), 2)
    picked = jnp.sum(jnp.where(hits, local_of(all_pivots)[:, :, None], 0), axis=1)
    rank = jnp.sum(jnp.where(same, counted[line:], 0), axis=0)
    code = (me - owner + line) % line * share + rank

    chips = line // CORES
    part = CORES * rhs_here // size
    update_partial, upper_all = pl.pallas_call(
        functools.partial(upper_kernel, size, line),
        out_shape=(
            jax.ShapeDtypeStruct((rhs_total, count_cols), BF16),
            jax.ShapeDtypeStruct((rhs_total, count_rows), BF16),
        ),
        in_specs=in_vmem(3),
        out_specs=tuple(in_vmem(2)),
        scratch_shapes=[
            pltpu.VMEM((line, rhs_here, count_cols), BF16),
            pltpu.VMEM((size, part, count_rows), F32),
            pltpu.VMEM((chips, part, count_rows), F32),
            pltpu.VMEM((chips, size, part, count_rows), BF16),
            pltpu.VMEM((chips, size - 1, part, count_rows), BF16),
            pltpu.VMEM((chips, size, part, count_rows), BF16),
        ]
        + [dma(chips - 1)] * 2
        + [dma(chips)] * 2
        + [dma(chips, size - 1)] * 4,
        compiler_params=params(0),
        name="upper",
    )(upper_rhs, inverse_pair[1], coupling_mat)
    upper_solved = lax.dynamic_slice_in_dim(upper_all, lax.axis_index("pcol") * own, own, 0)
    update = lax.psum_scatter(update_partial, "prow", scatter_dimension=0, tiled=True)
    lower_ready = (lower_rhs - update.astype(F32)).astype(BF16)
    later_pair, _ = lax.optimization_barrier((inverse_blocks, update_partial))
    later_inverse = later_pair[0].reshape(count_rows, count_cols)
    permuted = pl.pallas_call(
        functools.partial(lower_kernel, size, line),
        out_shape=jax.ShapeDtypeStruct((own, width), BF16),
        in_specs=in_vmem(5),
        out_specs=in_vmem(1)[0],
        scratch_shapes=sum_scratch(size, own, count_rows)
        + [
            pltpu.VMEM((line - 1, own, share), BF16),
            pltpu.VMEM((line, own, share), BF16),
            pltpu.VMEM((line, rhs_here, count_cols), BF16),
        ]
        + [dma(chips - 1)] * 2
        + [dma(chips)] * 2
        + [dma(PARTS, size - 1)] * 2
        + [dma(PARTS, line - 1)] * 2,
        compiler_params=params(1),
        name="lower",
    )(lower_ready, later_inverse, upper_solved, picked.reshape(line, 1, share), code.reshape(1, width))
    return permuted.reshape(own, pivots.shape[0], 1, tile_width)


def solution(mesh):
    in_specs = (
        P("prow", None, "pcol", None),
        P(None, None, "prow", None, None, "pcol", None),
        P(None, "prow", None, None, "pcol", None),
        P(None, "prow", None),
    )
    out_specs = P("pcol", None, "prow", None)
    return jax.shard_map(body, mesh=mesh, in_specs=in_specs, out_specs=out_specs, check_vma=False)
```

```python
import functools

import jax
import jax.numpy as jnp
from jax import lax
from jax.experimental import pallas as pl
from jax.experimental.pallas import tpu as pltpu
from jax.sharding import PartitionSpec as P

BF16 = jnp.bfloat16
F32 = jnp.float32
MESH = pl.DeviceIdType.MESH
CORES = 2
GROUPS = 2
BASE = 128
NT = (((1,), (1,)), ((), ()))
NN = (((1,), (0,)), ((), ()))


def tile_of(size):
    return 256 if size % 256 == 0 else 128


def span(index, size):
    return pl.ds(pl.multiple_of(index * size, size), size)


def chunks_of(rhs_here):
    return max(1, min(4, rhs_here // 16))


def window_kernel(
    size, line, chunks,
    rhs_ref, low_ref, later_ref, first_ref, coup_ref, code_ref, digit_ref, out_ref,
    gat_ref, low_gat_ref, mat_ref, coup_mat_ref, later_mat_ref, prod_ref, own_ref, send_ref,
    recv_ref, low_recv_ref, full_ref, keep_ref, give_ref, got_ref, pass_ref, run_ref,
    pick_ref, spot_ref, sel_ref, take_ref, ask_ref, asked_ref,
    copy_sem, slot_sem,
    down_s, down_r, up_s, up_r, pair_s, pair_r, pdown_s, pdown_r, pup_s, pup_r,
    sum_s, sum_r, share_s, share_r, core_s, core_r, run_s, run_r, back_s, back_r, bpair_s, bpair_r,
    move_s, move_r, ask_s, ask_r,
):
    chips = line // CORES
    here = lax.axis_index("prow")
    place = lax.axis_index("pcol")
    chip = here // CORES
    core = lax.rem(here, CORES)
    tiles, rhs_here, width = rhs_ref.shape
    hb = rhs_here // chunks
    rows = line * hb
    part = rows // size
    share = pick_ref.shape[2]
    depth = mat_ref.shape[0]
    count = out_ref.shape[2]
    tile = tile_of(depth)
    wide = tile_of(width)
    zg = chips // GROUPS
    pieces = [(c, g) for c in reversed(range(tiles)) for g in range(GROUPS)]
    peers = [lax.rem(place + step, size) for step in range(1, size)]
    above = lax.rem(here + CORES, line)
    below = lax.rem(here + line - CORES, line)
    partner = chip * CORES + (CORES - 1 - core)

    barrier = pltpu.get_barrier_semaphore()
    for step in range(1, line):
        pl.semaphore_signal(
            barrier, inc=1, device_id={"prow": lax.rem(here + step, line)}, device_id_type=MESH
        )
    for peer in peers:
        pl.semaphore_signal(barrier, inc=1, device_id={"pcol": peer}, device_id_type=MESH)
    pl.semaphore_wait(barrier, line - 1 + size - 1)

    def need(tile_index, at):
        return at * CORES <= tile_index * size + place

    needs = [need(c, chip) for c in range(tiles)]
    has_above = chip < chips - 1
    has_below = chip > 0
    feeds = [jnp.logical_and(has_above, need(c, chip + 1)) for c in range(tiles)]
    needed = sum(n.astype(jnp.int32) for n in needs)
    both = jnp.logical_and

    def remote(src, dst, sends, recvs, axis, device):
        return pltpu.make_async_remote_copy(
            src_ref=src, dst_ref=dst, send_sem=sends, recv_sem=recvs,
            device_id={axis: device}, device_id_type=MESH,
        )

    ends = []

    def begin(cond, copy):
        if cond is None:
            copy.start()
        else:
            pl.when(cond)(copy.start)
        ends.append((cond, copy))

    mats = [
        pltpu.make_async_copy(src, dst, copy_sem.at[i])
        for i, (src, dst) in enumerate(
            ((first_ref, mat_ref), (coup_ref, coup_mat_ref), (later_ref, later_mat_ref))
        )
    ]

    def mine(m):
        return rhs_ref.at[:, pl.ds(m * hb, hb)]

    def slots(m):
        return pltpu.make_async_copy(mine(m), gat_ref.at[m, :, chip, core], slot_sem.at[m])

    def down(m, k, block):
        src = mine(m) if k == 0 else gat_ref.at[m, :, block, core]
        return remote(
            src, gat_ref.at[m, :, block, core], down_s.at[m, k], down_r.at[m, k], "prow", below
        )

    def up(m, k, c, block):
        src = rhs_ref.at[c, pl.ds(m * hb, hb)] if k == 0 else gat_ref.at[m, c, block, core]
        return remote(
            src, gat_ref.at[m, c, block, core], up_s.at[m, k, c], up_r.at[m, k, c], "prow", above
        )

    def pair(m):
        return remote(
            mine(m), gat_ref.at[m, :, chip, core], pair_s.at[m], pair_r.at[m], "prow", partner
        )

    def pair_down(m, k, block):
        ref = gat_ref.at[m, :, block, core]
        return remote(ref, ref, pdown_s.at[m, k], pdown_r.at[m, k], "prow", partner)

    def pair_up(m, k, c, block):
        ref = gat_ref.at[m, c, block, core]
        return remote(ref, ref, pup_s.at[m, k, c], pup_r.at[m, k, c], "prow", partner)

    def gather_start(m):
        slots(m).start()
        begin(has_below, down(m, 0, chip))
        for c in reversed(range(tiles)):
            begin(feeds[c], up(m, 0, c, chip))
        begin(None, pair(m))

    def gather(m):
        for k in range(chips - 1):
            block = chip + 1 + k
            has = block < chips
            pl.when(has)(down(m, k, block).wait_recv)
            if k + 1 < chips - 1:
                begin(both(has, has_below), down(m, k + 1, block))
            begin(has, pair_down(m, k, block))
            block = chip - 1 - k
            has = block >= 0
            for c in reversed(range(tiles)):
                pl.when(both(has, needs[c]))(up(m, k, c, block).wait_recv)
                if k + 1 < chips - 1:
                    begin(both(has, feeds[c]), up(m, k + 1, c, block))
                begin(both(has, needs[c]), pair_up(m, k, c, block))
        slots(m).wait()
        pair(m).wait_recv()
        for k in range(chips - 1):
            block = chip + 1 + k
            pl.when(block < chips)(pair_down(m, k, block).wait_recv)
            block = chip - 1 - k
            for c in range(tiles):
                pl.when(both(block >= 0, needs[c]))(pair_up(m, k, c, block).wait_recv)

    def summed(stage, m, index):
        landing = recv_ref if stage == 0 else low_recv_ref
        return remote(
            send_ref.at[stage, m % 2, peers[index]], landing.at[m, index],
            sum_s.at[stage, m, index], sum_r.at[stage, m, index], "pcol", peers[index],
        )

    def multiply(stage, m):
        source = gat_ref if stage == 0 else low_gat_ref
        matrix = mat_ref if stage == 0 else later_mat_ref
        if m >= 2:
            for index in range(size - 1):
                summed(stage, m - 2, index).wait_send()
        for n in range(tiles + 1):

            @pl.when(needed == n)
            def _(n=n):
                @pl.loop(0, depth // tile)
                def _(step):
                    cols = span(step, tile)
                    value = jnp.zeros((rows, tile), F32)
                    for c in range(tiles - n, tiles):
                        value = value + lax.dot_general(
                            source[m, c].reshape(rows, width),
                            matrix[cols, c * width : (c + 1) * width],
                            NT,
                            preferred_element_type=F32,
                        )
                    for owner in range(size):
                        piece = value[owner * part : (owner + 1) * part]
                        prod_ref[owner, :, cols] = piece
                        send_ref[stage, m % 2, owner, :, cols] = piece.astype(BF16)

        for index in range(size - 1):
            summed(stage, m, index).start()
        own_ref[stage, m % 2] = prod_ref[place]

    def total_of(stage, m):
        landing = recv_ref if stage == 0 else low_recv_ref
        total = own_ref[stage, m % 2]
        for index in range(size - 1):
            summed(stage, m, index).wait_recv()
            total = total + landing[m, index].astype(F32)
        return total.astype(BF16)

    def shared(m, index):
        ref = full_ref.at[m, place]
        return remote(ref, ref, share_s.at[m, index], share_r.at[m, index], "pcol", peers[index])

    def settle(m):
        full_ref[m, place] = total_of(0, m)
        for index in range(size - 1):
            begin(None, shared(m, index))

    def crossed(m):
        return remote(
            give_ref.at[m % 2], got_ref.at[m], core_s.at[m], core_r.at[m], "prow", partner
        )

    def couple(m):
        for index in range(size - 1):
            shared(m, index).wait_recv()
        if m >= 2:
            crossed(m - 2).wait_send()
        for c in range(tiles):

            @pl.loop(0, width // wide)
            def _(step, c=c):
                value = lax.dot_general(
                    full_ref[m].reshape(rows, depth),
                    coup_mat_ref[:, pl.ds(pl.multiple_of(c * width + step * wide, wide), wide)],
                    NN,
                    preferred_element_type=F32,
                ).reshape(chips, CORES, hb, wide)
                cols = span(step, wide)
                for one in range(CORES):

                    @pl.when(core == one)
                    def _(one=one):
                        keep_ref[c, :, :, cols] = value[:, one]
                        give_ref[m % 2, c, :, :, cols] = value[:, 1 - one].astype(BF16)

        crossed(m).start()

    def running(m, j):
        c, g = pieces[j]
        group = pl.ds(g * zg, zg)
        return remote(
            pass_ref.at[m % 2, c, group], run_ref.at[m, c, group], run_s.at[m, j], run_r.at[m, j],
            "prow", below,
        )

    def back(m, j):
        c, g = pieces[j]
        ref = low_gat_ref.at[m, c, pl.ds(g * zg, zg), core]
        return remote(ref, ref, back_s.at[m, j], back_r.at[m, j], "prow", above)

    def back_pair(m, j):
        c, g = pieces[j]
        ref = low_gat_ref.at[m, c, pl.ds(g * zg, zg), core]
        return remote(ref, ref, bpair_s.at[m, j], bpair_r.at[m, j], "prow", partner)

    def reduce(m):
        crossed(m).wait_recv()
        for j, (c, g) in enumerate(pieces):
            if m >= 2:
                pl.when(has_below)(running(m - 2, j).wait_send)
            pl.when(has_above)(running(m, j).wait_recv)

            def combine(chained, final, c=c, g=g):
                for z in range(g * zg, (g + 1) * zg):
                    flag = jnp.where(chip == z, 1.0, 0.0).astype(F32)
                    value = low_ref[c, m * hb : (m + 1) * hb, :] * flag
                    value = value - (keep_ref[c, z] + got_ref[m, c, z].astype(F32))
                    if chained:
                        value = value + run_ref[m, c, z].astype(F32)
                    if final:
                        low_gat_ref[m, c, z, core] = value.astype(BF16)
                    else:
                        pass_ref[m % 2, c, z] = value.astype(BF16)

            pl.when(jnp.logical_not(has_above))(functools.partial(combine, False, False))
            pl.when(both(has_above, has_below))(functools.partial(combine, True, False))
            pl.when(jnp.logical_not(has_below))(functools.partial(combine, True, True))
            pl.when(has_below)(running(m, j).start)
            root = jnp.logical_not(has_below)
            begin(both(root, feeds[c]), back(m, j))
            begin(root, back_pair(m, j))

    def return_up(m, when):
        for j, (c, g) in enumerate(pieces):
            cond = both(both(has_below, needs[c]), when)
            pl.when(cond)(back(m, j).wait_recv)
            begin(both(cond, feeds[c]), back(m, j))
            begin(cond, back_pair(m, j))

    def lower(m):
        for j, (c, g) in enumerate(pieces):
            pl.when(needs[c])(back_pair(m, j).wait_recv)
        multiply(1, m)

    def ask(step):
        source = lax.rem(here + step, line)
        return remote(
            ask_ref.at[source], asked_ref.at[here], ask_s.at[step - 1], ask_r.at[step - 1],
            "prow", source,
        )

    def spots():
        ids = lax.broadcasted_iota(jnp.int32, (share, count), 0)

        @pl.loop(0, line)
        def _(source):
            hit = jnp.where(ids + source * share == code_ref[...], 1.0, 0.0).astype(BF16)
            spot_ref[span(source, share), :] = hit
            digits = lax.dot_general(digit_ref[...], hit, NT, preferred_element_type=F32)
            wanted = digits[0:1] * BASE + digits[1:2]
            ask_ref[source] = jnp.broadcast_to(wanted, (8, share))

        for step in range(1, line):
            begin(None, ask(step))
        asked_ref[here] = ask_ref[here]

    def picks():
        for step in range(1, line):
            ask(step).wait_recv()
        ids = lax.broadcasted_iota(jnp.int32, (2 * depth, share), 0)

        @pl.loop(0, line)
        def _(target):
            wanted = asked_ref[target][0:1].astype(jnp.int32)
            pick_ref[target] = jnp.where(ids == wanted, 1.0, 0.0).astype(BF16)

    def select_upper(m):
        @pl.loop(0, line)
        def _(target):
            sel_ref[m, target] = lax.dot_general(
                full_ref[m, place], pick_ref[target, depth:], NN, preferred_element_type=F32
            ).astype(BF16)

    def move(m, step):
        target = lax.rem(here + step, line)
        return remote(
            sel_ref.at[m, target], take_ref.at[m, :, span(here, share)],
            move_s.at[m, step - 1], move_r.at[m, step - 1], "prow", target,
        )

    def send_rows(m):
        solved = total_of(1, m)

        def chosen(target):
            low = lax.dot_general(
                solved, pick_ref[target, :depth], NN, preferred_element_type=F32
            )
            return (low + sel_ref[m, target].astype(F32)).astype(BF16)

        for step in range(1, line):
            target = lax.rem(here + step, line)
            sel_ref[m, target] = chosen(target)
            begin(None, move(m, step))
        take_ref[m, :, span(here, share)] = chosen(here)

    def put(m):
        for step in range(1, line):
            move(m, step).wait_recv()

        across = tile_of(count)

        @pl.loop(0, count // across)
        def _(step):
            cols = span(step, across)
            value = lax.dot_general(
                take_ref[m], spot_ref[:, cols], NN, preferred_element_type=F32
            ).astype(BF16)
            out_ref[:, m * hb : (m + 1) * hb, cols] = value.reshape(line // size, hb, across)

    for m in range(chunks):
        gather_start(m)
    for copy in mats:
        copy.start()
    spots()
    gather(0)
    for copy in mats:
        copy.wait()

    def valid(m):
        return 0 <= m < chunks

    last = chip == chips - 1
    for t in range(chunks + 4):
        if valid(t - 1):
            settle(t - 1)
        if valid(t):
            multiply(0, t)
        if t == 0:
            picks()
        if valid(t + 1):
            gather(t + 1)
        if valid(t - 1):
            couple(t - 1)
        if valid(t - 2):
            return_up(t - 2, jnp.logical_not(last))
        if valid(t - 1):
            reduce(t - 1)
        if valid(t - 2):
            return_up(t - 2, last)
        if valid(t - 1):
            select_upper(t - 1)
        if valid(t - 2):
            lower(t - 2)
        if valid(t - 3):
            send_rows(t - 3)
        if valid(t - 4):
            put(t - 4)
    for m in range(max(0, chunks - 2), chunks):
        for index in range(size - 1):
            summed(0, m, index).wait_send()
            summed(1, m, index).wait_send()
        crossed(m).wait_send()
        for j in range(len(pieces)):
            pl.when(has_below)(running(m, j).wait_send)
    for cond, copy in ends:
        if cond is None:
            copy.wait_send()
        else:
            pl.when(cond)(copy.wait_send)


def pair_of(*shape):
    return [pltpu.SemaphoreType.DMA(shape)] * 2


def body(right_side, inverse_blocks, coupling, pivots):
    rhs_here = right_side.shape[0]
    width = right_side.shape[3]
    depth = inverse_blocks.shape[1] * width
    tiles = inverse_blocks.shape[4]
    line = lax.axis_size("prow")
    size = lax.axis_size("pcol")
    chunks = chunks_of(rhs_here)
    chips = line // CORES
    hb = rhs_here // chunks
    rows = line * hb
    part = rows // size

    inverse_pair = inverse_blocks.reshape(2, depth, tiles * width)
    coupling_mat = coupling.reshape(depth, tiles * width)
    sides = right_side.reshape(rhs_here, 2 * tiles, width)
    lower_rhs = sides[:, :tiles].transpose(1, 0, 2)
    upper_rhs = sides[:, tiles:].astype(BF16).transpose(1, 0, 2)

    pivot = pivots.reshape(-1)
    count = pivot.shape[0]
    share = count // line
    owner = pivot // width % line
    local = pivot // (width * line) * width + pivot % width
    same = owner[None, :] == lax.broadcasted_iota(jnp.int32, (line, 1), 0)
    before = lax.broadcasted_iota(jnp.int32, (count, count), 0)
    after = lax.broadcasted_iota(jnp.int32, (count, count), 1)
    counted = jnp.dot(
        same.astype(BF16), (before < after).astype(BF16), preferred_element_type=F32
    )
    rank = jnp.sum(jnp.where(same, counted, 0.0), axis=0).astype(jnp.int32)
    code = owner * share + rank
    digit = lax.broadcasted_iota(jnp.int32, (16, 1), 0)
    digits = jnp.where(
        digit == 0, local // BASE, jnp.where(digit == 1, local % BASE, 0)
    ).astype(BF16)

    strip = (tiles, chips, hb, width)
    pieces = tiles * GROUPS
    vmem, anywhere = pl.BlockSpec(memory_space=pltpu.VMEM), pl.BlockSpec(memory_space=pl.ANY)
    permuted = pl.pallas_call(
        functools.partial(window_kernel, size, line, chunks),
        out_shape=jax.ShapeDtypeStruct((line // size, rhs_here, count), BF16),
        in_specs=[anywhere, vmem, anywhere, anywhere, anywhere, vmem, vmem],
        out_specs=vmem,
        scratch_shapes=[
            pltpu.VMEM((chunks, tiles, chips, CORES, hb, width), BF16),
            pltpu.VMEM((chunks, tiles, chips, CORES, hb, width), BF16),
            pltpu.VMEM((depth, tiles * width), BF16),
            pltpu.VMEM((depth, tiles * width), BF16),
            pltpu.VMEM((depth, tiles * width), BF16),
            pltpu.VMEM((size, part, depth), F32),
            pltpu.VMEM((2, 2, part, depth), F32),
            pltpu.VMEM((2, 2, size, part, depth), BF16),
            pltpu.VMEM((chunks, size - 1, part, depth), BF16),
            pltpu.VMEM((chunks, size - 1, part, depth), BF16),
            pltpu.VMEM((chunks, size, part, depth), BF16),
            pltpu.VMEM(strip, F32),
            pltpu.VMEM((2, *strip), BF16),
            pltpu.VMEM((chunks, *strip), BF16),
            pltpu.VMEM((2, *strip), BF16),
            pltpu.VMEM((chunks, *strip), BF16),
            pltpu.VMEM((line, 2 * depth, share), BF16),
            pltpu.VMEM((count, count), BF16),
            pltpu.VMEM((chunks, line, part, share), BF16),
            pltpu.VMEM((chunks, part, count), BF16),
            pltpu.VMEM((line, 8, share), F32),
            pltpu.VMEM((line, 8, share), F32),
            pltpu.SemaphoreType.DMA((3,)),
            pltpu.SemaphoreType.DMA((chunks,)),
        ]
        + pair_of(chunks, chips - 1)
        + pair_of(chunks, chips - 1, tiles)
        + pair_of(chunks)
        + pair_of(chunks, chips - 1)
        + pair_of(chunks, chips - 1, tiles)
        + pair_of(2, chunks, size - 1)
        + pair_of(chunks, size - 1)
        + pair_of(chunks)
        + pair_of(chunks, pieces)
        + pair_of(chunks, pieces)
        + pair_of(chunks, pieces)
        + pair_of(chunks, line - 1)
        + pair_of(line - 1),
        compiler_params=pltpu.CompilerParams(
            collective_id=0, has_side_effects=True, vmem_limit_bytes=62 * 1024 * 1024
        ),
        name="window",
    )(
        upper_rhs, lower_rhs, inverse_pair[0], inverse_pair[1], coupling_mat,
        code.reshape(1, count), digits,
    )
    return permuted.reshape(rhs_here * line // size, pivots.shape[0], 1, width)


def solution(mesh):
    in_specs = (
        P("prow", None, "pcol", None),
        P(None, None, "prow", None, None, "pcol", None),
        P(None, "prow", None, None, "pcol", None),
        P(None, "prow", None),
    )
    out_specs = P("pcol", None, "prow", None)
    return jax.shard_map(body, mesh=mesh, in_specs=in_specs, out_specs=out_specs, check_vma=False)
```

```python
import functools

import jax
import jax.numpy as jnp
from jax import lax
from jax.experimental import pallas as pl
from jax.experimental.pallas import tpu as pltpu
from jax.sharding import PartitionSpec as P

BF16 = jnp.bfloat16
F32 = jnp.float32
MESH = pl.DeviceIdType.MESH
CORES = 2
GROUPS = 2
BASE = 128
NT = (((1,), (1,)), ((), ()))
NN = (((1,), (0,)), ((), ()))


def tile_of(size):
    return 256 if size % 256 == 0 else 128


def span(index, size):
    return pl.ds(pl.multiple_of(index * size, size), size)


def chunks_of(rhs_here):
    return max(1, min(4, rhs_here // 16))


def window_kernel(
    size, line, chunks,
    rhs_ref, low_ref, inv_ref, coup_ref, code_ref, digit_ref, out_ref,
    gat_ref, low_gat_ref, mat_ref, coup_mat_ref, later_mat_ref, prod_ref, own_ref, send_ref,
    recv_ref, low_recv_ref, full_ref, keep_ref, give_ref, got_ref, pass_ref, run_ref, meet_ref,
    pick_ref, spot_ref, sel_ref, take_ref, ask_ref, asked_ref,
    copy_sem, slot_sem,
    down_s, down_r, up_s, up_r, pair_s, pair_r,
    sum_s, sum_r, share_s, share_r, core_s, core_r, run_s, run_r, back_s, back_r, fall_s, fall_r, bpair_s, bpair_r,
    move_s, move_r, ask_s, ask_r,
):
    chips = line // CORES
    here = lax.axis_index("prow")
    place = lax.axis_index("pcol")
    chip = here // CORES
    core = lax.rem(here, CORES)
    tiles, rhs_here, width = rhs_ref.shape
    hb = rhs_here // chunks
    rows = line * hb
    part = rows // size
    share = pick_ref.shape[2]
    depth = mat_ref.shape[0]
    count = out_ref.shape[2]
    tile = tile_of(depth)
    wide = tile_of(width)
    zg = chips // GROUPS
    pieces = [(c, g) for c in reversed(range(tiles)) for g in range(GROUPS)]
    peers = [lax.rem(place + step, size) for step in range(1, size)]
    above = lax.rem(here + CORES, line)
    below = lax.rem(here + line - CORES, line)
    partner = chip * CORES + (CORES - 1 - core)

    barrier = pltpu.get_barrier_semaphore()
    for step in range(1, line):
        pl.semaphore_signal(
            barrier, inc=1, device_id={"prow": lax.rem(here + step, line)}, device_id_type=MESH
        )
    for peer in peers:
        pl.semaphore_signal(barrier, inc=1, device_id={"pcol": peer}, device_id_type=MESH)
    pl.semaphore_wait(barrier, line - 1 + size - 1)

    def need(tile_index, at):
        return at * CORES <= tile_index * size + place

    needs = [need(c, chip) for c in range(tiles)]
    has_above = chip < chips - 1
    has_below = chip > 0
    feeds = [jnp.logical_and(has_above, need(c, chip + 1)) for c in range(tiles)]
    needed = sum(n.astype(jnp.int32) for n in needs)
    both = jnp.logical_and

    def remote(src, dst, sends, recvs, axis, device):
        return pltpu.make_async_remote_copy(
            src_ref=src, dst_ref=dst, send_sem=sends, recv_sem=recvs,
            device_id={axis: device}, device_id_type=MESH,
        )

    ends = []

    def begin(cond, copy):
        if cond is None:
            copy.start()
        else:
            pl.when(cond)(copy.start)
        ends.append((cond, copy))

    mats = [
        pltpu.make_async_copy(src, dst, copy_sem.at[i])
        for i, (src, dst) in enumerate(
            ((inv_ref.at[1], mat_ref), (coup_ref, coup_mat_ref), (inv_ref.at[0], later_mat_ref))
        )
    ]

    def mine(m):
        return rhs_ref.at[:, pl.ds(m * hb, hb)]

    def slots(m):
        return pltpu.make_async_copy(mine(m), gat_ref.at[m, :, chip, core], slot_sem.at[m])

    def spread(m, offset, c, sends, recvs):
        return remote(
            rhs_ref.at[c, pl.ds(m * hb, hb)], gat_ref.at[m, c, chip, core],
            sends.at[m, abs(offset) - 1, c], recvs.at[m, abs(offset) - 1, c], "prow",
            lax.rem(here + line + CORES * offset, line),
        )

    def pair(m, c):
        ref = gat_ref.at[m, c, :, core]
        return remote(ref, ref, pair_s.at[m, c], pair_r.at[m, c], "prow", partner)

    def gather_start(m):
        slots(m).start()
        for c in reversed(range(tiles)):
            for k in reversed(range(1, chips)):
                begin(both(chip >= k, need(c, chip - k)), spread(m, -k, c, down_s, down_r))
                begin(both(chip + k < chips, need(c, chip + k)), spread(m, k, c, up_s, up_r))

    def gather(m):
        slots(m).wait()
        for c in reversed(range(tiles)):
            for k in range(1, chips):
                pl.when(both(chip + k < chips, needs[c]))(spread(m, -k, c, down_s, down_r).wait_recv)
                pl.when(both(chip >= k, needs[c]))(spread(m, k, c, up_s, up_r).wait_recv)
            begin(needs[c], pair(m, c))

    def gathered(m):
        for c in range(tiles):
            pl.when(needs[c])(pair(m, c).wait_recv)

    def summed(stage, m, index):
        landing = recv_ref if stage == 0 else low_recv_ref
        return remote(
            send_ref.at[stage, m % 2, peers[index]], landing.at[m, index],
            sum_s.at[stage, m, index], sum_r.at[stage, m, index], "pcol", peers[index],
        )

    def multiply(stage, m):
        source = gat_ref if stage == 0 else low_gat_ref
        matrix = mat_ref if stage == 0 else later_mat_ref
        if m >= 2:
            for index in range(size - 1):
                summed(stage, m - 2, index).wait_send()
        for n in range(tiles + 1):

            @pl.when(needed == n)
            def _(n=n):
                @pl.loop(0, depth // tile)
                def _(step):
                    cols = span(step, tile)
                    value = jnp.zeros((rows, tile), F32)
                    for c in range(tiles - n, tiles):
                        value = value + lax.dot_general(
                            source[m, c].reshape(rows, width),
                            matrix[cols, c * width : (c + 1) * width],
                            NT,
                            preferred_element_type=F32,
                        )
                    for owner in range(size):
                        piece = value[owner * part : (owner + 1) * part]
                        prod_ref[owner, :, cols] = piece
                        send_ref[stage, m % 2, owner, :, cols] = piece.astype(BF16)

        for index in range(size - 1):
            summed(stage, m, index).start()
        own_ref[stage, m % 2] = prod_ref[place]

    def total_of(stage, m):
        landing = recv_ref if stage == 0 else low_recv_ref
        total = own_ref[stage, m % 2]
        for index in range(size - 1):
            summed(stage, m, index).wait_recv()
            total = total + landing[m, index].astype(F32)
        return total.astype(BF16)

    def shared(m, index):
        ref = full_ref.at[m, place]
        return remote(ref, ref, share_s.at[m, index], share_r.at[m, index], "pcol", peers[index])

    def settle(m):
        full_ref[m, place] = total_of(0, m)
        for index in range(size - 1):
            begin(None, shared(m, index))

    def crossed(m):
        return remote(
            give_ref.at[m % 2], got_ref.at[m], core_s.at[m], core_r.at[m], "prow", partner
        )

    def couple(m):
        for index in range(size - 1):
            shared(m, index).wait_recv()
        if m >= 2:
            crossed(m - 2).wait_send()
        for c in range(tiles):

            @pl.loop(0, width // wide)
            def _(step, c=c):
                value = lax.dot_general(
                    full_ref[m].reshape(rows, depth),
                    coup_mat_ref[:, pl.ds(pl.multiple_of(c * width + step * wide, wide), wide)],
                    NN,
                    preferred_element_type=F32,
                ).reshape(chips, CORES, hb, wide)
                cols = span(step, wide)
                for one in range(CORES):

                    @pl.when(core == one)
                    def _(one=one):
                        keep_ref[c, :, :, cols] = value[:, one]
                        give_ref[m % 2, c, :, :, cols] = value[:, 1 - one].astype(BF16)

        crossed(m).start()

    root = min(1, chips - 1)
    at_root = chip == root
    over = chip > root
    under = chip < root
    fed_above = both(chip >= root, has_above)
    fed_below = both(at_root, has_below)

    def running(m, j):
        c, g = pieces[j]
        group = pl.ds(g * zg, zg)
        return remote(
            pass_ref.at[m % 2, c, group], run_ref.at[m, c, group], run_s.at[m, j], run_r.at[m, j],
            "prow", below,
        )

    def rising(m, j):
        c, g = pieces[j]
        group = pl.ds(g * zg, zg)
        return remote(
            pass_ref.at[m % 2, c, group], meet_ref.at[m, c, group], run_s.at[m, j],
            fall_r.at[m, j], "prow", above,
        )

    def final(m, j):
        c, g = pieces[j]
        return low_gat_ref.at[m, c, pl.ds(g * zg, zg), core]

    def back(m, j):
        return remote(
            final(m, j), final(m, j), back_s.at[m, j], back_r.at[m, j], "prow", above
        )

    def fall(m, j):
        return remote(
            final(m, j), final(m, j), fall_s.at[m, j], back_r.at[m, j], "prow", below
        )

    def back_pair(m, j):
        return remote(
            final(m, j), final(m, j), bpair_s.at[m, j], bpair_r.at[m, j], "prow", partner
        )

    def passed(m, j):
        pl.when(over)(running(m, j).wait_send)
        pl.when(under)(rising(m, j).wait_send)

    def reduce(m):
        crossed(m).wait_recv()
        for j, (c, g) in enumerate(pieces):
            if m >= 2:
                passed(m - 2, j)
            pl.when(fed_above)(running(m, j).wait_recv)
            pl.when(fed_below)(rising(m, j).wait_recv)

            def combine(upper_sum, lower_sum, done, c=c, g=g):
                for z in range(g * zg, (g + 1) * zg):
                    flag = jnp.where(chip == z, 1.0, 0.0).astype(F32)
                    value = low_ref[c, m * hb : (m + 1) * hb, :] * flag
                    value = value - (keep_ref[c, z] + got_ref[m, c, z].astype(F32))
                    if upper_sum:
                        value = value + run_ref[m, c, z].astype(F32)
                    if lower_sum:
                        value = value + meet_ref[m, c, z].astype(F32)
                    if done:
                        low_gat_ref[m, c, z, core] = value.astype(BF16)
                    else:
                        pass_ref[m % 2, c, z] = value.astype(BF16)

            starts = jnp.logical_or(under, both(over, jnp.logical_not(has_above)))
            pl.when(starts)(functools.partial(combine, False, False, False))
            pl.when(both(over, has_above))(functools.partial(combine, True, False, False))
            pl.when(at_root)(functools.partial(combine, root < chips - 1, root > 0, True))
            pl.when(over)(running(m, j).start)
            pl.when(under)(rising(m, j).start)
            begin(both(at_root, feeds[c]), back(m, j))
            begin(both(at_root, has_below), fall(m, j))
            begin(both(at_root, needs[c]), back_pair(m, j))

    def come_back(m, when):
        for j, (c, g) in enumerate(pieces):
            cond = both(both(jnp.logical_not(at_root), needs[c]), when)
            pl.when(cond)(back(m, j).wait_recv)
            begin(both(both(cond, over), feeds[c]), back(m, j))
            begin(cond, back_pair(m, j))

    def lower(m):
        for j, (c, g) in enumerate(pieces):
            pl.when(needs[c])(back_pair(m, j).wait_recv)
        multiply(1, m)

    def ask(step):
        source = lax.rem(here + step, line)
        return remote(
            ask_ref.at[source], asked_ref.at[here], ask_s.at[step - 1], ask_r.at[step - 1],
            "prow", source,
        )

    def spots():
        ids = lax.broadcasted_iota(jnp.int32, (share, count), 0)

        @pl.loop(0, line)
        def _(source):
            hit = jnp.where(ids + source * share == code_ref[...], 1.0, 0.0).astype(BF16)
            spot_ref[span(source, share), :] = hit
            digits = lax.dot_general(digit_ref[...], hit, NT, preferred_element_type=F32)
            wanted = digits[0:1] * BASE + digits[1:2]
            ask_ref[source] = jnp.broadcast_to(wanted, (8, share))

        for step in range(1, line):
            begin(None, ask(step))
        asked_ref[here] = ask_ref[here]

    def picks():
        for step in range(1, line):
            ask(step).wait_recv()
        ids = lax.broadcasted_iota(jnp.int32, (2 * depth, share), 0)

        @pl.loop(0, line)
        def _(target):
            wanted = asked_ref[target][0:1].astype(jnp.int32)
            pick_ref[target] = jnp.where(ids == wanted, 1.0, 0.0).astype(BF16)

    def select_upper(m):
        @pl.loop(0, line)
        def _(target):
            sel_ref[m, target] = lax.dot_general(
                full_ref[m, place], pick_ref[target, depth:], NN, preferred_element_type=F32
            ).astype(BF16)

    def move(m, step):
        target = lax.rem(here + step, line)
        return remote(
            sel_ref.at[m, target], take_ref.at[m, :, span(here, share)],
            move_s.at[m, step - 1], move_r.at[m, step - 1], "prow", target,
        )

    def send_rows(m):
        solved = total_of(1, m)

        def chosen(target):
            low = lax.dot_general(
                solved, pick_ref[target, :depth], NN, preferred_element_type=F32
            )
            return (low + sel_ref[m, target].astype(F32)).astype(BF16)

        for step in range(1, line):
            target = lax.rem(here + step, line)
            sel_ref[m, target] = chosen(target)
            begin(None, move(m, step))
        take_ref[m, :, span(here, share)] = chosen(here)

    def put(m):
        for step in range(1, line):
            move(m, step).wait_recv()

        across = tile_of(count)

        @pl.loop(0, count // across)
        def _(step):
            cols = span(step, across)
            value = lax.dot_general(
                take_ref[m], spot_ref[:, cols], NN, preferred_element_type=F32
            ).astype(BF16)
            out_ref[:, m * hb : (m + 1) * hb, cols] = value.reshape(line // size, hb, across)

    for m in range(chunks):
        gather_start(m)
    for copy in mats:
        copy.start()
    spots()
    gather(0)
    for copy in mats:
        copy.wait()

    def valid(m):
        return 0 <= m < chunks

    far = chip > root + 1
    for t in range(chunks + 5):
        if valid(t - 1):
            settle(t - 1)
        if valid(t):
            gathered(t)
            multiply(0, t)
        if t == 0:
            picks()
        if valid(t + 1):
            gather(t + 1)
        if valid(t - 1):
            couple(t - 1)
        if valid(t - 2):
            come_back(t - 2, jnp.logical_not(far))
        if valid(t - 1):
            reduce(t - 1)
        if valid(t - 1):
            select_upper(t - 1)
        if valid(t - 3):
            come_back(t - 3, far)
            lower(t - 3)
        if valid(t - 4):
            send_rows(t - 4)
        if valid(t - 5):
            put(t - 5)
    for m in range(max(0, chunks - 2), chunks):
        for index in range(size - 1):
            summed(0, m, index).wait_send()
            summed(1, m, index).wait_send()
        crossed(m).wait_send()
        for j in range(len(pieces)):
            passed(m, j)
    for cond, copy in ends:
        if cond is None:
            copy.wait_send()
        else:
            pl.when(cond)(copy.wait_send)


def pair_of(*shape):
    return [pltpu.SemaphoreType.DMA(shape)] * 2


def body(right_side, inverse_blocks, coupling, pivots):
    rhs_here = right_side.shape[0]
    width = right_side.shape[3]
    depth = inverse_blocks.shape[1] * width
    tiles = inverse_blocks.shape[4]
    line = lax.axis_size("prow")
    size = lax.axis_size("pcol")
    chunks = chunks_of(rhs_here)
    chips = line // CORES
    hb = rhs_here // chunks
    rows = line * hb
    part = rows // size

    inverse_pair = inverse_blocks.reshape(2, depth, tiles * width)
    coupling_mat = coupling.reshape(depth, tiles * width)
    sides = right_side.reshape(rhs_here, 2 * tiles, width)
    lower_rhs = sides[:, :tiles].transpose(1, 0, 2)
    upper_rhs = sides[:, tiles:].astype(BF16).transpose(1, 0, 2)

    pivot = pivots.reshape(-1)
    count = pivot.shape[0]
    share = count // line
    owner = pivot // width % line
    local = pivot // (width * line) * width + pivot % width
    same = owner[None, :] == lax.broadcasted_iota(jnp.int32, (line, 1), 0)
    before = lax.broadcasted_iota(jnp.int32, (count, count), 0)
    after = lax.broadcasted_iota(jnp.int32, (count, count), 1)
    counted = jnp.dot(
        same.astype(BF16), (before < after).astype(BF16), preferred_element_type=F32
    )
    rank = jnp.sum(jnp.where(same, counted, 0.0), axis=0).astype(jnp.int32)
    code = owner * share + rank
    digit = lax.broadcasted_iota(jnp.int32, (16, 1), 0)
    digits = jnp.where(
        digit == 0, local // BASE, jnp.where(digit == 1, local % BASE, 0)
    ).astype(BF16)

    strip = (tiles, chips, hb, width)
    pieces = tiles * GROUPS
    vmem, anywhere = pl.BlockSpec(memory_space=pltpu.VMEM), pl.BlockSpec(memory_space=pl.ANY)
    permuted = pl.pallas_call(
        functools.partial(window_kernel, size, line, chunks),
        out_shape=jax.ShapeDtypeStruct((line // size, rhs_here, count), BF16),
        in_specs=[anywhere, vmem, anywhere, anywhere, vmem, vmem],
        out_specs=vmem,
        scratch_shapes=[
            pltpu.VMEM((chunks, tiles, chips, CORES, hb, width), BF16),
            pltpu.VMEM((chunks, tiles, chips, CORES, hb, width), BF16),
            pltpu.VMEM((depth, tiles * width), BF16),
            pltpu.VMEM((depth, tiles * width), BF16),
            pltpu.VMEM((depth, tiles * width), BF16),
            pltpu.VMEM((size, part, depth), F32),
            pltpu.VMEM((2, 2, part, depth), F32),
            pltpu.VMEM((2, 2, size, part, depth), BF16),
            pltpu.VMEM((chunks, size - 1, part, depth), BF16),
            pltpu.VMEM((chunks, size - 1, part, depth), BF16),
            pltpu.VMEM((chunks, size, part, depth), BF16),
            pltpu.VMEM(strip, F32),
            pltpu.VMEM((2, *strip), BF16),
            pltpu.VMEM((chunks, *strip), BF16),
            pltpu.VMEM((2, *strip), BF16),
            pltpu.VMEM((chunks, *strip), BF16),
            pltpu.VMEM((chunks, *strip), BF16),
            pltpu.VMEM((line, 2 * depth, share), BF16),
            pltpu.VMEM((count, count), BF16),
            pltpu.VMEM((chunks, line, part, share), BF16),
            pltpu.VMEM((chunks, part, count), BF16),
            pltpu.VMEM((line, 8, share), F32),
            pltpu.VMEM((line, 8, share), F32),
            pltpu.SemaphoreType.DMA((3,)),
            pltpu.SemaphoreType.DMA((chunks,)),
        ]
        + pair_of(chunks, chips - 1, tiles)
        + pair_of(chunks, chips - 1, tiles)
        + pair_of(chunks, tiles)
        + pair_of(2, chunks, size - 1)
        + pair_of(chunks, size - 1)
        + pair_of(chunks)
        + pair_of(chunks, pieces)
        + pair_of(chunks, pieces)
        + pair_of(chunks, pieces)
        + pair_of(chunks, pieces)
        + pair_of(chunks, line - 1)
        + pair_of(line - 1),
        compiler_params=pltpu.CompilerParams(
            collective_id=0, has_side_effects=True, vmem_limit_bytes=62 * 1024 * 1024
        ),
        name="window",
    )(
        upper_rhs, lower_rhs, inverse_pair, coupling_mat,
        code.reshape(1, count), digits,
    )
    return permuted.reshape(rhs_here * line // size, pivots.shape[0], 1, width)


def solution(mesh):
    in_specs = (
        P("prow", None, "pcol", None),
        P(None, None, "prow", None, None, "pcol", None),
        P(None, "prow", None, None, "pcol", None),
        P(None, "prow", None),
    )
    out_specs = P("pcol", None, "prow", None)
    return jax.shard_map(body, mesh=mesh, in_specs=in_specs, out_specs=out_specs, check_vma=False)
```

```python
import functools

import jax
import jax.numpy as jnp
from jax import lax
from jax.experimental import pallas as pl
from jax.experimental.pallas import tpu as pltpu
from jax.sharding import PartitionSpec as P

BF16 = jnp.bfloat16
F32 = jnp.float32
MESH = pl.DeviceIdType.MESH
CORES = 2
GROUPS = 2
BASE = 128
NEAR = 1
NT = (((1,), (1,)), ((), ()))
NN = (((1,), (0,)), ((), ()))


def tile_of(size):
    return 256 if size % 256 == 0 else 128


def span(index, size):
    return pl.ds(pl.multiple_of(index * size, size), size)


def chunks_of(rhs_here):
    return max(1, min(4, rhs_here // 16))


def window_kernel(
    size, line, chunks,
    rhs_ref, fell_ref, rose_ref, low_ref, later_ref, first_ref, coup_ref, code_ref, digit_ref, out_ref,
    gat_ref, low_gat_ref, mat_ref, coup_mat_ref, later_mat_ref, prod_ref, own_ref, send_ref,
    recv_ref, low_recv_ref, full_ref, keep_ref, give_ref, got_ref, pass_ref, run_ref, meet_ref,
    pick_ref, spot_ref, sel_ref, take_ref, ask_ref, asked_ref,
    copy_sem, slot_sem,
    down_s, down_r, up_s, up_r, pair_s, pair_r,
    sum_s, sum_r, share_s, share_r, core_s, core_r, run_s, run_r, back_s, back_r, fall_s, fall_r, bpair_s, bpair_r,
    move_s, move_r, ask_s, ask_r,
):
    chips = line // CORES
    here = lax.axis_index("prow")
    place = lax.axis_index("pcol")
    chip = here // CORES
    core = lax.rem(here, CORES)
    tiles, rhs_here, width = rhs_ref.shape
    hb = rhs_here // chunks
    rows = line * hb
    part = rows // size
    share = pick_ref.shape[2]
    depth = mat_ref.shape[0]
    count = out_ref.shape[2]
    tile = tile_of(depth)
    wide = tile_of(width)
    zg = chips // GROUPS
    pieces = [(c, g) for c in reversed(range(tiles)) for g in range(GROUPS)]
    peers = [lax.rem(place + step, size) for step in range(1, size)]
    above = lax.rem(here + CORES, line)
    below = lax.rem(here + line - CORES, line)
    partner = chip * CORES + (CORES - 1 - core)

    barrier = pltpu.get_barrier_semaphore()
    for step in range(1, line):
        pl.semaphore_signal(
            barrier, inc=1, device_id={"prow": lax.rem(here + step, line)}, device_id_type=MESH
        )
    for peer in peers:
        pl.semaphore_signal(barrier, inc=1, device_id={"pcol": peer}, device_id_type=MESH)
    pl.semaphore_wait(barrier, line - 1 + size - 1)

    def need(tile_index, at):
        return at * CORES <= tile_index * size + place

    needs = [need(c, chip) for c in range(tiles)]
    has_above = chip < chips - 1
    has_below = chip > 0
    feeds = [jnp.logical_and(has_above, need(c, chip + 1)) for c in range(tiles)]
    needed = sum(n.astype(jnp.int32) for n in needs)
    both = jnp.logical_and

    def remote(src, dst, sends, recvs, axis, device):
        return pltpu.make_async_remote_copy(
            src_ref=src, dst_ref=dst, send_sem=sends, recv_sem=recvs,
            device_id={axis: device}, device_id_type=MESH,
        )

    ends = []

    def begin(cond, copy):
        if cond is None:
            copy.start()
        else:
            pl.when(cond)(copy.start)
        ends.append((cond, copy))

    mats = [
        pltpu.make_async_copy(src, dst, copy_sem.at[i])
        for i, (src, dst) in enumerate(
            ((first_ref, mat_ref), (coup_ref, coup_mat_ref), (later_ref, later_mat_ref))
        )
    ]

    arrived = [(0, rhs_ref), (1, fell_ref), (-1, rose_ref)]

    def slots(m):
        for index, (offset, ref) in enumerate(arrived):
            block = chip + offset
            copy = pltpu.make_async_copy(
                ref.at[:, pl.ds(m * hb, hb)], gat_ref.at[m, :, block, core], slot_sem.at[m, index]
            )
            yield both(block >= 0, block < chips), copy

    def spread(m, offset, c, sends, recvs):
        return remote(
            rhs_ref.at[c, pl.ds(m * hb, hb)], gat_ref.at[m, c, chip, core],
            sends.at[m, abs(offset) - 1 - NEAR, c], recvs.at[m, abs(offset) - 1 - NEAR, c], "prow",
            lax.rem(here + line + CORES * offset, line),
        )

    def pair(m, c):
        ref = gat_ref.at[m, c, :, core]
        return remote(ref, ref, pair_s.at[m, c], pair_r.at[m, c], "prow", partner)

    def gather_start(m):
        for cond, copy in slots(m):
            pl.when(cond)(copy.start)
        for c in reversed(range(tiles)):
            for k in reversed(range(1 + NEAR, chips)):
                begin(both(chip >= k, need(c, chip - k)), spread(m, -k, c, down_s, down_r))
                begin(both(chip + k < chips, need(c, chip + k)), spread(m, k, c, up_s, up_r))

    def gather(m):
        for cond, copy in slots(m):
            pl.when(cond)(copy.wait)
        for c in reversed(range(tiles)):
            for k in range(1 + NEAR, chips):
                pl.when(both(chip + k < chips, needs[c]))(spread(m, -k, c, down_s, down_r).wait_recv)
                pl.when(both(chip >= k, needs[c]))(spread(m, k, c, up_s, up_r).wait_recv)
            begin(needs[c], pair(m, c))

    def gathered(m):
        for c in range(tiles):
            pl.when(needs[c])(pair(m, c).wait_recv)

    def summed(stage, m, index):
        landing = recv_ref if stage == 0 else low_recv_ref
        return remote(
            send_ref.at[stage, m % 2, peers[index]], landing.at[m, index],
            sum_s.at[stage, m, index], sum_r.at[stage, m, index], "pcol", peers[index],
        )

    def multiply(stage, m):
        source = gat_ref if stage == 0 else low_gat_ref
        matrix = mat_ref if stage == 0 else later_mat_ref
        if m >= 2:
            for index in range(size - 1):
                summed(stage, m - 2, index).wait_send()
        for n in range(tiles + 1):

            @pl.when(needed == n)
            def _(n=n):
                @pl.loop(0, depth // tile)
                def _(step):
                    cols = span(step, tile)
                    value = jnp.zeros((rows, tile), F32)
                    for c in range(tiles - n, tiles):
                        value = value + lax.dot_general(
                            source[m, c].reshape(rows, width),
                            matrix[cols, c * width : (c + 1) * width],
                            NT,
                            preferred_element_type=F32,
                        )
                    for owner in range(size):
                        piece = value[owner * part : (owner + 1) * part]
                        prod_ref[owner, :, cols] = piece
                        send_ref[stage, m % 2, owner, :, cols] = piece.astype(BF16)

        for index in range(size - 1):
            summed(stage, m, index).start()
        own_ref[stage, m % 2] = prod_ref[place]

    def total_of(stage, m):
        landing = recv_ref if stage == 0 else low_recv_ref
        total = own_ref[stage, m % 2]
        for index in range(size - 1):
            summed(stage, m, index).wait_recv()
            total = total + landing[m, index].astype(F32)
        return total.astype(BF16)

    def shared(m, index):
        ref = full_ref.at[m, place]
        return remote(ref, ref, share_s.at[m, index], share_r.at[m, index], "pcol", peers[index])

    def settle(m):
        full_ref[m, place] = total_of(0, m)
        for index in range(size - 1):
            begin(None, shared(m, index))

    def crossed(m):
        return remote(
            give_ref.at[m % 2], got_ref.at[m], core_s.at[m], core_r.at[m], "prow", partner
        )

    def couple(m):
        for index in range(size - 1):
            shared(m, index).wait_recv()
        if m >= 2:
            crossed(m - 2).wait_send()
        for c in range(tiles):

            @pl.loop(0, width // wide)
            def _(step, c=c):
                value = lax.dot_general(
                    full_ref[m].reshape(rows, depth),
                    coup_mat_ref[:, pl.ds(pl.multiple_of(c * width + step * wide, wide), wide)],
                    NN,
                    preferred_element_type=F32,
                ).reshape(chips, CORES, hb, wide)
                cols = span(step, wide)
                for one in range(CORES):

                    @pl.when(core == one)
                    def _(one=one):
                        keep_ref[c, :, :, cols] = value[:, one]
                        give_ref[m % 2, c, :, :, cols] = value[:, 1 - one].astype(BF16)

        crossed(m).start()

    root = min(1, chips - 1)
    at_root = chip == root
    over = chip > root
    under = chip < root
    fed_above = both(chip >= root, has_above)
    fed_below = both(at_root, has_below)

    def running(m, j):
        c, g = pieces[j]
        group = pl.ds(g * zg, zg)
        return remote(
            pass_ref.at[m % 2, c, group], run_ref.at[m, c, group], run_s.at[m, j], run_r.at[m, j],
            "prow", below,
        )

    def rising(m, j):
        c, g = pieces[j]
        group = pl.ds(g * zg, zg)
        return remote(
            pass_ref.at[m % 2, c, group], meet_ref.at[m, c, group], run_s.at[m, j],
            fall_r.at[m, j], "prow", above,
        )

    def final(m, j):
        c, g = pieces[j]
        return low_gat_ref.at[m, c, pl.ds(g * zg, zg), core]

    def back(m, j):
        return remote(
            final(m, j), final(m, j), back_s.at[m, j], back_r.at[m, j], "prow", above
        )

    def fall(m, j):
        return remote(
            final(m, j), final(m, j), fall_s.at[m, j], back_r.at[m, j], "prow", below
        )

    def back_pair(m, j):
        return remote(
            final(m, j), final(m, j), bpair_s.at[m, j], bpair_r.at[m, j], "prow", partner
        )

    def passed(m, j):
        pl.when(over)(running(m, j).wait_send)
        pl.when(under)(rising(m, j).wait_send)

    def reduce(m):
        crossed(m).wait_recv()
        for j, (c, g) in enumerate(pieces):
            if m >= 2:
                passed(m - 2, j)
            pl.when(fed_above)(running(m, j).wait_recv)
            pl.when(fed_below)(rising(m, j).wait_recv)

            def combine(upper_sum, lower_sum, done, c=c, g=g):
                for z in range(g * zg, (g + 1) * zg):
                    flag = jnp.where(chip == z, 1.0, 0.0).astype(F32)
                    value = low_ref[c, m * hb : (m + 1) * hb, :] * flag
                    value = value - (keep_ref[c, z] + got_ref[m, c, z].astype(F32))
                    if upper_sum:
                        value = value + run_ref[m, c, z].astype(F32)
                    if lower_sum:
                        value = value + meet_ref[m, c, z].astype(F32)
                    if done:
                        low_gat_ref[m, c, z, core] = value.astype(BF16)
                    else:
                        pass_ref[m % 2, c, z] = value.astype(BF16)

            starts = jnp.logical_or(under, both(over, jnp.logical_not(has_above)))
            pl.when(starts)(functools.partial(combine, False, False, False))
            pl.when(both(over, has_above))(functools.partial(combine, True, False, False))
            pl.when(at_root)(functools.partial(combine, root < chips - 1, root > 0, True))
            pl.when(over)(running(m, j).start)
            pl.when(under)(rising(m, j).start)
            begin(both(at_root, feeds[c]), back(m, j))
            begin(both(at_root, has_below), fall(m, j))
            begin(both(at_root, needs[c]), back_pair(m, j))

    def come_back(m, when):
        for j, (c, g) in enumerate(pieces):
            cond = both(both(jnp.logical_not(at_root), needs[c]), when)
            pl.when(cond)(back(m, j).wait_recv)
            begin(both(both(cond, over), feeds[c]), back(m, j))
            begin(cond, back_pair(m, j))

    def lower(m):
        for j, (c, g) in enumerate(pieces):
            pl.when(needs[c])(back_pair(m, j).wait_recv)
        multiply(1, m)

    def ask(step):
        source = lax.rem(here + step, line)
        return remote(
            ask_ref.at[source], asked_ref.at[here], ask_s.at[step - 1], ask_r.at[step - 1],
            "prow", source,
        )

    def spots():
        ids = lax.broadcasted_iota(jnp.int32, (share, count), 0)

        @pl.loop(0, line)
        def _(source):
            hit = jnp.where(ids + source * share == code_ref[...], 1.0, 0.0).astype(BF16)
            spot_ref[span(source, share), :] = hit
            digits = lax.dot_general(digit_ref[...], hit, NT, preferred_element_type=F32)
            wanted = digits[0:1] * BASE + digits[1:2]
            ask_ref[source] = jnp.broadcast_to(wanted, (8, share))

        for step in range(1, line):
            begin(None, ask(step))
        asked_ref[here] = ask_ref[here]

    def picks():
        for step in range(1, line):
            ask(step).wait_recv()
        ids = lax.broadcasted_iota(jnp.int32, (2 * depth, share), 0)

        @pl.loop(0, line)
        def _(target):
            wanted = asked_ref[target][0:1].astype(jnp.int32)
            pick_ref[target] = jnp.where(ids == wanted, 1.0, 0.0).astype(BF16)

    def select_upper(m):
        @pl.loop(0, line)
        def _(target):
            sel_ref[m, target] = lax.dot_general(
                full_ref[m, place], pick_ref[target, depth:], NN, preferred_element_type=F32
            ).astype(BF16)

    def move(m, step):
        target = lax.rem(here + step, line)
        return remote(
            sel_ref.at[m, target], take_ref.at[m, :, span(here, share)],
            move_s.at[m, step - 1], move_r.at[m, step - 1], "prow", target,
        )

    def send_rows(m):
        solved = total_of(1, m)

        def chosen(target):
            low = lax.dot_general(
                solved, pick_ref[target, :depth], NN, preferred_element_type=F32
            )
            return (low + sel_ref[m, target].astype(F32)).astype(BF16)

        for step in range(1, line):
            target = lax.rem(here + step, line)
            sel_ref[m, target] = chosen(target)
            begin(None, move(m, step))
        take_ref[m, :, span(here, share)] = chosen(here)

    def put(m):
        for step in range(1, line):
            move(m, step).wait_recv()

        across = tile_of(count)

        @pl.loop(0, count // across)
        def _(step):
            cols = span(step, across)
            value = lax.dot_general(
                take_ref[m], spot_ref[:, cols], NN, preferred_element_type=F32
            ).astype(BF16)
            out_ref[:, m * hb : (m + 1) * hb, cols] = value.reshape(line // size, hb, across)

    gather_start(0)
    for copy in mats:
        copy.start()
    spots()
    gather(0)
    if chunks > 1:
        gather_start(1)
    for copy in mats:
        copy.wait()

    def valid(m):
        return 0 <= m < chunks

    far = chip > root + 1
    for t in range(chunks + 7):
        if valid(t - 1):
            settle(t - 1)
        if valid(t):
            gathered(t)
            multiply(0, t)
        if t == 0:
            picks()
        if valid(t - 3):
            come_back(t - 3, far)
        if valid(t - 3):
            lower(t - 3)
        if valid(t - 4):
            send_rows(t - 4)
        if valid(t - 5):
            put(t - 5)
        if valid(t + 1):
            gather(t + 1)
        if valid(t + 2):
            gather_start(t + 2)
        if valid(t - 1):
            couple(t - 1)
        if valid(t - 1):
            select_upper(t - 1)
        if valid(t - 2):
            come_back(t - 2, jnp.logical_not(far))
        if valid(t - 1):
            reduce(t - 1)
    for m in range(max(0, chunks - 2), chunks):
        for index in range(size - 1):
            summed(0, m, index).wait_send()
            summed(1, m, index).wait_send()
        crossed(m).wait_send()
        for j in range(len(pieces)):
            passed(m, j)
    for cond, copy in ends:
        if cond is None:
            copy.wait_send()
        else:
            pl.when(cond)(copy.wait_send)


def pair_of(*shape):
    return [pltpu.SemaphoreType.DMA(shape)] * 2


def body(right_side, inverse_blocks, coupling, pivots):
    rhs_here = right_side.shape[0]
    width = right_side.shape[3]
    depth = inverse_blocks.shape[1] * width
    tiles = inverse_blocks.shape[4]
    line = lax.axis_size("prow")
    size = lax.axis_size("pcol")
    chunks = chunks_of(rhs_here)
    chips = line // CORES
    hb = rhs_here // chunks
    rows = line * hb
    part = rows // size

    coupling_mat = coupling.reshape(depth, tiles * width)
    sides = right_side.reshape(rhs_here, 2 * tiles, width)
    lower_rhs = sides[:, :tiles].transpose(1, 0, 2)
    upper_rhs = sides[:, tiles:].astype(BF16).transpose(1, 0, 2)

    downward = [(p, p - CORES) for p in range(CORES, line)]
    upward = [(p - CORES, p) for p in range(CORES, line)]
    fell = lax.ppermute(upper_rhs, "prow", downward)
    rose = lax.ppermute(upper_rhs, "prow", upward)
    first = inverse_blocks[1].reshape(depth, tiles * width)
    other, _ = lax.optimization_barrier((inverse_blocks, upper_rhs))
    later = other[0].reshape(depth, tiles * width)
    pivot = pivots.reshape(-1)
    count = pivot.shape[0]
    share = count // line
    owner = pivot // width % line
    local = pivot // (width * line) * width + pivot % width
    same = owner[None, :] == lax.broadcasted_iota(jnp.int32, (line, 1), 0)
    before = lax.broadcasted_iota(jnp.int32, (count, count), 0)
    after = lax.broadcasted_iota(jnp.int32, (count, count), 1)
    counted = jnp.dot(
        same.astype(BF16), (before < after).astype(BF16), preferred_element_type=F32
    )
    rank = jnp.sum(jnp.where(same, counted, 0.0), axis=0).astype(jnp.int32)
    code = owner * share + rank
    digit = lax.broadcasted_iota(jnp.int32, (16, 1), 0)
    digits = jnp.where(
        digit == 0, local // BASE, jnp.where(digit == 1, local % BASE, 0)
    ).astype(BF16)

    strip = (tiles, chips, hb, width)
    pieces = tiles * GROUPS
    vmem, anywhere = pl.BlockSpec(memory_space=pltpu.VMEM), pl.BlockSpec(memory_space=pl.ANY)
    permuted = pl.pallas_call(
        functools.partial(window_kernel, size, line, chunks),
        out_shape=jax.ShapeDtypeStruct((line // size, rhs_here, count), BF16),
        in_specs=[anywhere] * 3 + [vmem] + [anywhere] * 3 + [vmem] * 2,
        out_specs=vmem,
        scratch_shapes=[
            pltpu.VMEM((chunks, tiles, chips, CORES, hb, width), BF16),
            pltpu.VMEM((chunks, tiles, chips, CORES, hb, width), BF16),
            pltpu.VMEM((depth, tiles * width), BF16),
            pltpu.VMEM((depth, tiles * width), BF16),
            pltpu.VMEM((depth, tiles * width), BF16),
            pltpu.VMEM((size, part, depth), F32),
            pltpu.VMEM((2, 2, part, depth), F32),
            pltpu.VMEM((2, 2, size, part, depth), BF16),
            pltpu.VMEM((chunks, size - 1, part, depth), BF16),
            pltpu.VMEM((chunks, size - 1, part, depth), BF16),
            pltpu.VMEM((chunks, size, part, depth), BF16),
            pltpu.VMEM(strip, F32),
            pltpu.VMEM((2, *strip), BF16),
            pltpu.VMEM((chunks, *strip), BF16),
            pltpu.VMEM((2, *strip), BF16),
            pltpu.VMEM((chunks, *strip), BF16),
            pltpu.VMEM((chunks, *strip), BF16),
            pltpu.VMEM((line, 2 * depth, share), BF16),
            pltpu.VMEM((count, count), BF16),
            pltpu.VMEM((chunks, line, part, share), BF16),
            pltpu.VMEM((chunks, part, count), BF16),
            pltpu.VMEM((line, 8, share), F32),
            pltpu.VMEM((line, 8, share), F32),
            pltpu.SemaphoreType.DMA((3,)),
            pltpu.SemaphoreType.DMA((chunks, 1 + 2 * NEAR)),
        ]
        + pair_of(chunks, max(1, chips - 1 - NEAR), tiles)
        + pair_of(chunks, max(1, chips - 1 - NEAR), tiles)
        + pair_of(chunks, tiles)
        + pair_of(2, chunks, size - 1)
        + pair_of(chunks, size - 1)
        + pair_of(chunks)
        + pair_of(chunks, pieces)
        + pair_of(chunks, pieces)
        + pair_of(chunks, pieces)
        + pair_of(chunks, pieces)
        + pair_of(chunks, line - 1)
        + pair_of(line - 1),
        compiler_params=pltpu.CompilerParams(
            collective_id=0, has_side_effects=True, vmem_limit_bytes=62 * 1024 * 1024
        ),
        name="window",
    )(
        upper_rhs, fell, rose, lower_rhs, later, first, coupling_mat,
        code.reshape(1, count), digits,
    )
    return permuted.reshape(rhs_here * line // size, pivots.shape[0], 1, width)


def solution(mesh):
    in_specs = (
        P("prow", None, "pcol", None),
        P(None, None, "prow", None, None, "pcol", None),
        P(None, "prow", None, None, "pcol", None),
        P(None, "prow", None),
    )
    out_specs = P("pcol", None, "prow", None)
    return jax.shard_map(body, mesh=mesh, in_specs=in_specs, out_specs=out_specs, check_vma=False)
```

```python
import functools

import jax
import jax.numpy as jnp
from jax import lax
from jax.experimental import pallas as pl
from jax.experimental.pallas import tpu as pltpu
from jax.sharding import PartitionSpec as P

BF16 = jnp.bfloat16
F32 = jnp.float32
MESH = pl.DeviceIdType.MESH
CORES = 2
GROUPS = 2
BASE = 128
NT = (((1,), (1,)), ((), ()))
NN = (((1,), (0,)), ((), ()))


def tile_of(size):
    return 256 if size % 256 == 0 else 128


def span(index, size):
    return pl.ds(pl.multiple_of(index * size, size), size)


def chunks_of(rhs_here):
    return max(1, min(4, rhs_here // 16))


def window_kernel(
    size, line, chunks,
    rhs_ref, fell_ref, rose_ref, low_ref, later_ref, first_ref, coup_ref, code_ref, digit_ref, out_ref,
    gat_ref, low_gat_ref, mat_ref, coup_mat_ref, later_mat_ref, prod_ref, own_ref, send_ref,
    recv_ref, low_recv_ref, full_ref, keep_ref, give_ref, got_ref, pass_ref, run_ref, meet_ref,
    pick_ref, spot_ref, sel_ref, take_ref, ask_ref, asked_ref,
    copy_sem, slot_sem,
    down_s, down_r, up_s, up_r, pair_s, pair_r,
    sum_s, sum_r, share_s, share_r, core_s, core_r, run_s, run_r, back_s, back_r, fall_s, fall_r, bpair_s, bpair_r,
    move_s, move_r, ask_s, ask_r,
):
    chips = line // CORES
    here = lax.axis_index("prow")
    place = lax.axis_index("pcol")
    chip = here // CORES
    core = lax.rem(here, CORES)
    tiles, rhs_here, width = rhs_ref.shape
    hb = rhs_here // chunks
    rows = line * hb
    part = rows // size
    share = pick_ref.shape[2]
    depth = mat_ref.shape[0]
    count = out_ref.shape[2]
    tile = tile_of(depth)
    wide = tile_of(width)
    zg = chips // GROUPS
    pieces = [(c, g) for c in reversed(range(tiles)) for g in range(GROUPS)]
    peers = [lax.rem(place + step, size) for step in range(1, size)]
    above = lax.rem(here + CORES, line)
    below = lax.rem(here + line - CORES, line)
    partner = chip * CORES + (CORES - 1 - core)

    barrier = pltpu.get_barrier_semaphore()
    for step in range(1, line):
        pl.semaphore_signal(
            barrier, inc=1, device_id={"prow": lax.rem(here + step, line)}, device_id_type=MESH
        )
    for peer in peers:
        pl.semaphore_signal(barrier, inc=1, device_id={"pcol": peer}, device_id_type=MESH)
    pl.semaphore_wait(barrier, line - 1 + size - 1)

    def need(tile_index, at):
        return at * CORES <= tile_index * size + place

    needs = [need(c, chip) for c in range(tiles)]
    has_above = chip < chips - 1
    has_below = chip > 0
    feeds = [jnp.logical_and(has_above, need(c, chip + 1)) for c in range(tiles)]
    needed = sum(n.astype(jnp.int32) for n in needs)
    both = jnp.logical_and

    def remote(src, dst, sends, recvs, axis, device):
        return pltpu.make_async_remote_copy(
            src_ref=src, dst_ref=dst, send_sem=sends, recv_sem=recvs,
            device_id={axis: device}, device_id_type=MESH,
        )

    ends = []

    def begin(cond, copy):
        if cond is None:
            copy.start()
        else:
            pl.when(cond)(copy.start)
        ends.append((cond, copy))

    mats = [
        pltpu.make_async_copy(src, dst, copy_sem.at[i])
        for i, (src, dst) in enumerate(
            ((first_ref, mat_ref), (coup_ref, coup_mat_ref), (later_ref, later_mat_ref))
        )
    ]

    arrived = [(0, rhs_ref), (1, fell_ref), (-1, rose_ref)]

    def slots(m):
        for index, (offset, ref) in enumerate(arrived):
            block = chip + offset
            copy = pltpu.make_async_copy(
                ref.at[:, pl.ds(m * hb, hb)], gat_ref.at[m, :, block, core], slot_sem.at[m, index]
            )
            yield both(block >= 0, block < chips), copy

    def spread(m, offset, c, sends, recvs):
        block, ref = (chip + 1, fell_ref) if offset < 0 else (chip - 1, rose_ref)
        return remote(
            ref.at[c, pl.ds(m * hb, hb)], gat_ref.at[m, c, block, core],
            sends.at[m, abs(offset) - 1, c], recvs.at[m, abs(offset) - 1, c], "prow",
            lax.rem(here + line + CORES * offset, line),
        )

    def pair(m, c):
        ref = gat_ref.at[m, c, :, core]
        return remote(ref, ref, pair_s.at[m, c], pair_r.at[m, c], "prow", partner)

    def gather_start(m):
        for cond, copy in slots(m):
            pl.when(cond)(copy.start)
        for c in reversed(range(tiles)):
            for k in reversed(range(1, chips - 1)):
                lower = both(chip >= k, has_above)
                begin(both(lower, need(c, chip - k)), spread(m, -k, c, down_s, down_r))
                upper = both(chip + k < chips, has_below)
                begin(both(upper, need(c, chip + k)), spread(m, k, c, up_s, up_r))

    def gather(m):
        for cond, copy in slots(m):
            pl.when(cond)(copy.wait)
        for c in reversed(range(tiles)):
            for k in range(1, chips - 1):
                lower = both(chip + k + 1 < chips, needs[c])
                pl.when(lower)(spread(m, -k, c, down_s, down_r).wait_recv)
                upper = both(chip >= k + 1, needs[c])
                pl.when(upper)(spread(m, k, c, up_s, up_r).wait_recv)
            begin(needs[c], pair(m, c))

    def gathered(m):
        for c in range(tiles):
            pl.when(needs[c])(pair(m, c).wait_recv)

    def summed(stage, m, index):
        landing = recv_ref if stage == 0 else low_recv_ref
        return remote(
            send_ref.at[stage, m % 2, peers[index]], landing.at[m, index],
            sum_s.at[stage, m, index], sum_r.at[stage, m, index], "pcol", peers[index],
        )

    def multiply(stage, m):
        source = gat_ref if stage == 0 else low_gat_ref
        matrix = mat_ref if stage == 0 else later_mat_ref
        if m >= 2:
            for index in range(size - 1):
                summed(stage, m - 2, index).wait_send()
        for n in range(tiles + 1):

            @pl.when(needed == n)
            def _(n=n):
                @pl.loop(0, depth // tile)
                def _(step):
                    cols = span(step, tile)
                    value = jnp.zeros((rows, tile), F32)
                    for c in range(tiles - n, tiles):
                        value = value + lax.dot_general(
                            source[m, c].reshape(rows, width),
                            matrix[cols, c * width : (c + 1) * width],
                            NT,
                            preferred_element_type=F32,
                        )
                    for owner in range(size):
                        piece = value[owner * part : (owner + 1) * part]
                        prod_ref[owner, :, cols] = piece
                        send_ref[stage, m % 2, owner, :, cols] = piece.astype(BF16)

        for index in range(size - 1):
            summed(stage, m, index).start()
        own_ref[stage, m % 2] = prod_ref[place]

    def total_of(stage, m):
        landing = recv_ref if stage == 0 else low_recv_ref
        total = own_ref[stage, m % 2]
        for index in range(size - 1):
            summed(stage, m, index).wait_recv()
            total = total + landing[m, index].astype(F32)
        return total.astype(BF16)

    def shared(m, index):
        ref = full_ref.at[m, place]
        return remote(ref, ref, share_s.at[m, index], share_r.at[m, index], "pcol", peers[index])

    def settle(m):
        full_ref[m, place] = total_of(0, m)
        for index in range(size - 1):
            begin(None, shared(m, index))

    def crossed(m):
        return remote(
            give_ref.at[m % 2], got_ref.at[m], core_s.at[m], core_r.at[m], "prow", partner
        )

    def couple(m):
        for index in range(size - 1):
            shared(m, index).wait_recv()
        if m >= 2:
            crossed(m - 2).wait_send()
        for c in range(tiles):

            @pl.loop(0, width // wide)
            def _(step, c=c):
                value = lax.dot_general(
                    full_ref[m].reshape(rows, depth),
                    coup_mat_ref[:, pl.ds(pl.multiple_of(c * width + step * wide, wide), wide)],
                    NN,
                    preferred_element_type=F32,
                ).reshape(chips, CORES, hb, wide)
                cols = span(step, wide)
                for one in range(CORES):

                    @pl.when(core == one)
                    def _(one=one):
                        keep_ref[c, :, :, cols] = value[:, one]
                        give_ref[m % 2, c, :, :, cols] = value[:, 1 - one].astype(BF16)

        crossed(m).start()

    root = min(1, chips - 1)
    at_root = chip == root
    over = chip > root
    under = chip < root
    fed_above = both(chip >= root, has_above)
    fed_below = both(at_root, has_below)

    def running(m, j):
        c, g = pieces[j]
        group = pl.ds(g * zg, zg)
        return remote(
            pass_ref.at[m % 2, c, group], run_ref.at[m, c, group], run_s.at[m, j], run_r.at[m, j],
            "prow", below,
        )

    def rising(m, j):
        c, g = pieces[j]
        group = pl.ds(g * zg, zg)
        return remote(
            pass_ref.at[m % 2, c, group], meet_ref.at[m, c, group], run_s.at[m, j],
            fall_r.at[m, j], "prow", above,
        )

    def final(m, j):
        c, g = pieces[j]
        return low_gat_ref.at[m, c, pl.ds(g * zg, zg), core]

    def back(m, j):
        return remote(
            final(m, j), final(m, j), back_s.at[m, j], back_r.at[m, j], "prow", above
        )

    def fall(m, j):
        return remote(
            final(m, j), final(m, j), fall_s.at[m, j], back_r.at[m, j], "prow", below
        )

    def back_pair(m, j):
        return remote(
            final(m, j), final(m, j), bpair_s.at[m, j], bpair_r.at[m, j], "prow", partner
        )

    def passed(m, j):
        pl.when(over)(running(m, j).wait_send)
        pl.when(under)(rising(m, j).wait_send)

    def reduce(m):
        crossed(m).wait_recv()
        for j, (c, g) in enumerate(pieces):
            if m >= 2:
                passed(m - 2, j)
            pl.when(fed_above)(running(m, j).wait_recv)
            pl.when(fed_below)(rising(m, j).wait_recv)

            def combine(upper_sum, lower_sum, done, c=c, g=g):
                for z in range(g * zg, (g + 1) * zg):
                    flag = jnp.where(chip == z, 1.0, 0.0).astype(F32)
                    value = low_ref[c, m * hb : (m + 1) * hb, :] * flag
                    value = value - (keep_ref[c, z] + got_ref[m, c, z].astype(F32))
                    if upper_sum:
                        value = value + run_ref[m, c, z].astype(F32)
                    if lower_sum:
                        value = value + meet_ref[m, c, z].astype(F32)
                    if done:
                        low_gat_ref[m, c, z, core] = value.astype(BF16)
                    else:
                        pass_ref[m % 2, c, z] = value.astype(BF16)

            starts = jnp.logical_or(under, both(over, jnp.logical_not(has_above)))
            pl.when(starts)(functools.partial(combine, False, False, False))
            pl.when(both(over, has_above))(functools.partial(combine, True, False, False))
            pl.when(at_root)(functools.partial(combine, root < chips - 1, root > 0, True))
            pl.when(over)(running(m, j).start)
            pl.when(under)(rising(m, j).start)
            begin(both(at_root, feeds[c]), back(m, j))
            begin(both(at_root, has_below), fall(m, j))
            begin(both(at_root, needs[c]), back_pair(m, j))

    def come_back(m, when):
        for j, (c, g) in enumerate(pieces):
            cond = both(both(jnp.logical_not(at_root), needs[c]), when)
            pl.when(cond)(back(m, j).wait_recv)
            begin(both(both(cond, over), feeds[c]), back(m, j))
            begin(cond, back_pair(m, j))

    def lower(m):
        for j, (c, g) in enumerate(pieces):
            pl.when(needs[c])(back_pair(m, j).wait_recv)
        multiply(1, m)

    def ask(step):
        source = lax.rem(here + step, line)
        return remote(
            ask_ref.at[source], asked_ref.at[here], ask_s.at[step - 1], ask_r.at[step - 1],
            "prow", source,
        )

    def spots():
        ids = lax.broadcasted_iota(jnp.int32, (share, count), 0)

        @pl.loop(0, line)
        def _(source):
            hit = jnp.where(ids + source * share == code_ref[...], 1.0, 0.0).astype(BF16)
            spot_ref[span(source, share), :] = hit
            digits = lax.dot_general(digit_ref[...], hit, NT, preferred_element_type=F32)
            wanted = digits[0:1] * BASE + digits[1:2]
            ask_ref[source] = jnp.broadcast_to(wanted, (8, share))

        for step in range(1, line):
            begin(None, ask(step))
        asked_ref[here] = ask_ref[here]

    def picks():
        for step in range(1, line):
            ask(step).wait_recv()
        ids = lax.broadcasted_iota(jnp.int32, (2 * depth, share), 0)

        @pl.loop(0, line)
        def _(target):
            wanted = asked_ref[target][0:1].astype(jnp.int32)
            pick_ref[target] = jnp.where(ids == wanted, 1.0, 0.0).astype(BF16)

    def select_upper(m):
        @pl.loop(0, line)
        def _(target):
            sel_ref[m, target] = lax.dot_general(
                full_ref[m, place], pick_ref[target, depth:], NN, preferred_element_type=F32
            ).astype(BF16)

    def move(m, step):
        target = lax.rem(here + step, line)
        return remote(
            sel_ref.at[m, target], take_ref.at[m, :, span(here, share)],
            move_s.at[m, step - 1], move_r.at[m, step - 1], "prow", target,
        )

    def send_rows(m):
        solved = total_of(1, m)

        def chosen(target):
            low = lax.dot_general(
                solved, pick_ref[target, :depth], NN, preferred_element_type=F32
            )
            return (low + sel_ref[m, target].astype(F32)).astype(BF16)

        for step in range(1, line):
            target = lax.rem(here + step, line)
            sel_ref[m, target] = chosen(target)
            begin(None, move(m, step))
        take_ref[m, :, span(here, share)] = chosen(here)

    def put(m):
        for step in range(1, line):
            move(m, step).wait_recv()

        across = tile_of(count)

        @pl.loop(0, count // across)
        def _(step):
            cols = span(step, across)
            value = lax.dot_general(
                take_ref[m], spot_ref[:, cols], NN, preferred_element_type=F32
            ).astype(BF16)
            out_ref[:, m * hb : (m + 1) * hb, cols] = value.reshape(line // size, hb, across)

    gather_start(0)
    for copy in mats:
        copy.start()
    spots()
    gather(0)
    if chunks > 1:
        gather_start(1)
    for copy in mats:
        copy.wait()

    def valid(m):
        return 0 <= m < chunks

    far = chip > root + 1
    for t in range(chunks + 7):
        if valid(t - 1):
            settle(t - 1)
        if valid(t):
            gathered(t)
            multiply(0, t)
        if t == 0:
            picks()
        if valid(t - 3):
            come_back(t - 3, far)
        if valid(t - 3):
            lower(t - 3)
        if valid(t - 4):
            send_rows(t - 4)
        if valid(t - 5):
            put(t - 5)
        if valid(t + 1):
            gather(t + 1)
        if valid(t + 2):
            gather_start(t + 2)
        if valid(t - 1):
            couple(t - 1)
        if valid(t - 1):
            select_upper(t - 1)
        if valid(t - 2):
            come_back(t - 2, jnp.logical_not(far))
        if valid(t - 1):
            reduce(t - 1)
    for m in range(max(0, chunks - 2), chunks):
        for index in range(size - 1):
            summed(0, m, index).wait_send()
            summed(1, m, index).wait_send()
        crossed(m).wait_send()
        for j in range(len(pieces)):
            passed(m, j)
    for cond, copy in ends:
        if cond is None:
            copy.wait_send()
        else:
            pl.when(cond)(copy.wait_send)


def pair_of(*shape):
    return [pltpu.SemaphoreType.DMA(shape)] * 2


def body(right_side, inverse_blocks, coupling, pivots):
    rhs_here = right_side.shape[0]
    width = right_side.shape[3]
    depth = inverse_blocks.shape[1] * width
    tiles = inverse_blocks.shape[4]
    line = lax.axis_size("prow")
    size = lax.axis_size("pcol")
    chunks = chunks_of(rhs_here)
    chips = line // CORES
    hb = rhs_here // chunks
    rows = line * hb
    part = rows // size

    coupling_mat = coupling.reshape(depth, tiles * width)
    sides = right_side.reshape(rhs_here, 2 * tiles, width)
    lower_rhs = sides[:, :tiles].transpose(1, 0, 2)
    upper_rhs = sides[:, tiles:].astype(BF16).transpose(1, 0, 2)

    downward = [(p, p - CORES) for p in range(CORES, line)]
    upward = [(p - CORES, p) for p in range(CORES, line)]
    fell = lax.ppermute(upper_rhs, "prow", downward)
    rose = lax.ppermute(upper_rhs, "prow", upward)
    first = inverse_blocks[1].reshape(depth, tiles * width)
    other, _ = lax.optimization_barrier((inverse_blocks, upper_rhs))
    later = other[0].reshape(depth, tiles * width)
    pivot = pivots.reshape(-1)
    count = pivot.shape[0]
    share = count // line
    owner = pivot // width % line
    local = pivot // (width * line) * width + pivot % width
    same = owner[None, :] == lax.broadcasted_iota(jnp.int32, (line, 1), 0)
    before = lax.broadcasted_iota(jnp.int32, (count, count), 0)
    after = lax.broadcasted_iota(jnp.int32, (count, count), 1)
    counted = jnp.dot(
        same.astype(BF16), (before < after).astype(BF16), preferred_element_type=F32
    )
    rank = jnp.sum(jnp.where(same, counted, 0.0), axis=0).astype(jnp.int32)
    code = owner * share + rank
    digit = lax.broadcasted_iota(jnp.int32, (16, 1), 0)
    digits = jnp.where(
        digit == 0, local // BASE, jnp.where(digit == 1, local % BASE, 0)
    ).astype(BF16)

    strip = (tiles, chips, hb, width)
    pieces = tiles * GROUPS
    vmem, anywhere = pl.BlockSpec(memory_space=pltpu.VMEM), pl.BlockSpec(memory_space=pl.ANY)
    permuted = pl.pallas_call(
        functools.partial(window_kernel, size, line, chunks),
        out_shape=jax.ShapeDtypeStruct((line // size, rhs_here, count), BF16),
        in_specs=[anywhere] * 3 + [vmem] + [anywhere] * 3 + [vmem] * 2,
        out_specs=vmem,
        scratch_shapes=[
            pltpu.VMEM((chunks, tiles, chips, CORES, hb, width), BF16),
            pltpu.VMEM((chunks, tiles, chips, CORES, hb, width), BF16),
            pltpu.VMEM((depth, tiles * width), BF16),
            pltpu.VMEM((depth, tiles * width), BF16),
            pltpu.VMEM((depth, tiles * width), BF16),
            pltpu.VMEM((size, part, depth), F32),
            pltpu.VMEM((2, 2, part, depth), F32),
            pltpu.VMEM((2, 2, size, part, depth), BF16),
            pltpu.VMEM((chunks, size - 1, part, depth), BF16),
            pltpu.VMEM((chunks, size - 1, part, depth), BF16),
            pltpu.VMEM((chunks, size, part, depth), BF16),
            pltpu.VMEM(strip, F32),
            pltpu.VMEM((2, *strip), BF16),
            pltpu.VMEM((chunks, *strip), BF16),
            pltpu.VMEM((2, *strip), BF16),
            pltpu.VMEM((chunks, *strip), BF16),
            pltpu.VMEM((chunks, *strip), BF16),
            pltpu.VMEM((line, 2 * depth, share), BF16),
            pltpu.VMEM((count, count), BF16),
            pltpu.VMEM((chunks, line, part, share), BF16),
            pltpu.VMEM((chunks, part, count), BF16),
            pltpu.VMEM((line, 8, share), F32),
            pltpu.VMEM((line, 8, share), F32),
            pltpu.SemaphoreType.DMA((3,)),
            pltpu.SemaphoreType.DMA((chunks, 3)),
        ]
        + pair_of(chunks, max(1, chips - 2), tiles)
        + pair_of(chunks, max(1, chips - 2), tiles)
        + pair_of(chunks, tiles)
        + pair_of(2, chunks, size - 1)
        + pair_of(chunks, size - 1)
        + pair_of(chunks)
        + pair_of(chunks, pieces)
        + pair_of(chunks, pieces)
        + pair_of(chunks, pieces)
        + pair_of(chunks, pieces)
        + pair_of(chunks, line - 1)
        + pair_of(line - 1),
        compiler_params=pltpu.CompilerParams(
            collective_id=0, has_side_effects=True, vmem_limit_bytes=62 * 1024 * 1024
        ),
        name="window",
    )(
        upper_rhs, fell, rose, lower_rhs, later, first, coupling_mat,
        code.reshape(1, count), digits,
    )
    return permuted.reshape(rhs_here * line // size, pivots.shape[0], 1, width)


def solution(mesh):
    in_specs = (
        P("prow", None, "pcol", None),
        P(None, None, "prow", None, None, "pcol", None),
        P(None, "prow", None, None, "pcol", None),
        P(None, "prow", None),
    )
    out_specs = P("pcol", None, "prow", None)
    return jax.shard_map(body, mesh=mesh, in_specs=in_specs, out_specs=out_specs, check_vma=False)
```

```python
import functools

import jax
import jax.numpy as jnp
from jax import lax
from jax.experimental import pallas as pl
from jax.experimental.pallas import tpu as pltpu
from jax.sharding import PartitionSpec as P

BF16 = jnp.bfloat16
F32 = jnp.float32
MESH = pl.DeviceIdType.MESH
CORES = 2
GROUPS = 2
BASE = 128
NT = (((1,), (1,)), ((), ()))
NN = (((1,), (0,)), ((), ()))


def tile_of(size):
    return 256 if size % 256 == 0 else 128


def span(index, size):
    return pl.ds(pl.multiple_of(index * size, size), size)


def chunks_of(rhs_here):
    return max(1, min(4, rhs_here // 16))


def window_kernel(
    size, line, chunks,
    rhs_ref, fell_ref, low_ref, later_ref, first_ref, coup_ref, code_ref, digit_ref, out_ref,
    gat_ref, low_gat_ref, mat_ref, coup_mat_ref, later_mat_ref, prod_ref, own_ref, send_ref,
    recv_ref, low_recv_ref, full_ref, keep_ref, give_ref, got_ref, pass_ref, run_ref, meet_ref,
    pick_ref, spot_ref, sel_ref, take_ref, ask_ref, asked_ref,
    raw_ref, copy_sem, slot_sem,
    down_s, down_r, up_s, up_r, pair_s, pair_r,
    sum_s, sum_r, share_s, share_r, core_s, core_r, run_s, run_r, back_s, back_r, fall_s, fall_r, bpair_s, bpair_r,
    move_s, move_r, ask_s, ask_r,
):
    chips = line // CORES
    here = lax.axis_index("prow")
    place = lax.axis_index("pcol")
    chip = here // CORES
    core = lax.rem(here, CORES)
    tiles, rhs_here, width = rhs_ref.shape
    hb = rhs_here // chunks
    rows = line * hb
    part = rows // size
    share = pick_ref.shape[2]
    depth = mat_ref.shape[0]
    count = out_ref.shape[2]
    tile = tile_of(depth)
    wide = tile_of(width)
    zg = chips // GROUPS
    pieces = [(c, g) for c in reversed(range(tiles)) for g in range(GROUPS)]
    peers = [lax.rem(place + step, size) for step in range(1, size)]
    above = lax.rem(here + CORES, line)
    below = lax.rem(here + line - CORES, line)
    partner = chip * CORES + (CORES - 1 - core)

    barrier = pltpu.get_barrier_semaphore()
    for step in range(1, line):
        pl.semaphore_signal(
            barrier, inc=1, device_id={"prow": lax.rem(here + step, line)}, device_id_type=MESH
        )
    for peer in peers:
        pl.semaphore_signal(barrier, inc=1, device_id={"pcol": peer}, device_id_type=MESH)
    pl.semaphore_wait(barrier, line - 1 + size - 1)

    def need(tile_index, at):
        return at * CORES <= tile_index * size + place

    needs = [need(c, chip) for c in range(tiles)]
    has_above = chip < chips - 1
    has_below = chip > 0
    feeds = [jnp.logical_and(has_above, need(c, chip + 1)) for c in range(tiles)]
    needed = sum(n.astype(jnp.int32) for n in needs)
    both = jnp.logical_and

    def remote(src, dst, sends, recvs, axis, device):
        return pltpu.make_async_remote_copy(
            src_ref=src, dst_ref=dst, send_sem=sends, recv_sem=recvs,
            device_id={axis: device}, device_id_type=MESH,
        )

    ends = []

    def begin(cond, copy):
        if cond is None:
            copy.start()
        else:
            pl.when(cond)(copy.start)
        ends.append((cond, copy))

    mats = [
        pltpu.make_async_copy(first_ref, mat_ref, copy_sem.at[0]),
        pltpu.make_async_copy(later_ref, later_mat_ref, copy_sem.at[1]),
    ]
    half = depth // 2

    def raw(index):
        return pltpu.make_async_copy(
            coup_ref.at[pl.ds(index * half, half)], raw_ref, copy_sem.at[2 + index]
        )

    def lay(index):
        raw(index).wait()

        @pl.loop(0, half // 64)
        def _(step):
            block = raw_ref[span(step, 64)]
            target = pl.ds(pl.multiple_of(index * half + step * 64, 64), 64)
            for c in range(tiles):
                coup_mat_ref[target, c * width : (c + 1) * width] = block[:, c, :]

        if index == 0:
            raw(1).start()

    arrived = [(0, rhs_ref), (1, fell_ref)]

    def slots(m):
        for index, (offset, ref) in enumerate(arrived):
            block = chip + offset
            copy = pltpu.make_async_copy(
                ref.at[:, pl.ds(m * hb, hb)], gat_ref.at[m, :, block, core], slot_sem.at[m, index]
            )
            yield both(block >= 0, block < chips), copy

    def spread(m, offset, c, sends, recvs):
        block, ref = (chip + 1, fell_ref) if offset < 0 else (chip, rhs_ref)
        return remote(
            ref.at[c, pl.ds(m * hb, hb)], gat_ref.at[m, c, block, core],
            sends.at[m, abs(offset) - 1, c], recvs.at[m, abs(offset) - 1, c], "prow",
            lax.rem(here + line + CORES * offset, line),
        )

    def pair(m, c):
        ref = gat_ref.at[m, c, :, core]
        return remote(ref, ref, pair_s.at[m, c], pair_r.at[m, c], "prow", partner)

    def gather_start(m):
        for cond, copy in slots(m):
            pl.when(cond)(copy.start)
        for c in reversed(range(tiles)):
            for k in reversed(range(1, chips - 1)):
                lower = both(chip >= k, has_above)
                begin(both(lower, need(c, chip - k)), spread(m, -k, c, down_s, down_r))
            for k in reversed(range(1, chips)):
                upper = both(chip + k < chips, need(c, chip + k))
                begin(upper, spread(m, k, c, up_s, up_r))

    def gather(m):
        for cond, copy in slots(m):
            pl.when(cond)(copy.wait)
        for c in reversed(range(tiles)):
            for k in range(1, chips - 1):
                lower = both(chip + k + 1 < chips, needs[c])
                pl.when(lower)(spread(m, -k, c, down_s, down_r).wait_recv)
            for k in range(1, chips):
                upper = both(chip >= k, needs[c])
                pl.when(upper)(spread(m, k, c, up_s, up_r).wait_recv)
            begin(needs[c], pair(m, c))

    def gathered(m):
        for c in range(tiles):
            pl.when(needs[c])(pair(m, c).wait_recv)

    def summed(stage, m, index):
        landing = recv_ref if stage == 0 else low_recv_ref
        return remote(
            send_ref.at[stage, m % 2, peers[index]], landing.at[m, index],
            sum_s.at[stage, m, index], sum_r.at[stage, m, index], "pcol", peers[index],
        )

    def multiply(stage, m):
        source = gat_ref if stage == 0 else low_gat_ref
        matrix = mat_ref if stage == 0 else later_mat_ref
        if m >= 2:
            for index in range(size - 1):
                summed(stage, m - 2, index).wait_send()
        for n in range(tiles + 1):

            @pl.when(needed == n)
            def _(n=n):
                @pl.loop(0, depth // tile)
                def _(step):
                    cols = span(step, tile)
                    value = jnp.zeros((rows, tile), F32)
                    for c in range(tiles - n, tiles):
                        value = value + lax.dot_general(
                            source[m, c].reshape(rows, width),
                            matrix[cols, c * width : (c + 1) * width],
                            NT,
                            preferred_element_type=F32,
                        )
                    for owner in range(size):
                        piece = value[owner * part : (owner + 1) * part]
                        prod_ref[owner, :, cols] = piece
                        send_ref[stage, m % 2, owner, :, cols] = piece.astype(BF16)

        for index in range(size - 1):
            summed(stage, m, index).start()
        own_ref[stage, m % 2] = prod_ref[place]

    def total_of(stage, m):
        landing = recv_ref if stage == 0 else low_recv_ref
        total = own_ref[stage, m % 2]
        for index in range(size - 1):
            summed(stage, m, index).wait_recv()
            total = total + landing[m, index].astype(F32)
        return total.astype(BF16)

    def shared(m, index):
        ref = full_ref.at[m, place]
        return remote(ref, ref, share_s.at[m, index], share_r.at[m, index], "pcol", peers[index])

    def settle(m):
        full_ref[m, place] = total_of(0, m)
        for index in range(size - 1):
            begin(None, shared(m, index))

    def crossed(m):
        return remote(
            give_ref.at[m % 2], got_ref.at[m], core_s.at[m], core_r.at[m], "prow", partner
        )

    def couple(m):
        for index in range(size - 1):
            shared(m, index).wait_recv()
        if m >= 2:
            crossed(m - 2).wait_send()
        for c in range(tiles):

            @pl.loop(0, width // wide)
            def _(step, c=c):
                value = lax.dot_general(
                    full_ref[m].reshape(rows, depth),
                    coup_mat_ref[:, pl.ds(pl.multiple_of(c * width + step * wide, wide), wide)],
                    NN,
                    preferred_element_type=F32,
                ).reshape(chips, CORES, hb, wide)
                cols = span(step, wide)
                for one in range(CORES):

                    @pl.when(core == one)
                    def _(one=one):
                        keep_ref[c, :, :, cols] = value[:, one]
                        give_ref[m % 2, c, :, :, cols] = value[:, 1 - one].astype(BF16)

        crossed(m).start()

    root = min(1, chips - 1)
    at_root = chip == root
    over = chip > root
    under = chip < root
    fed_above = both(chip >= root, has_above)
    fed_below = both(at_root, has_below)

    def running(m, j):
        c, g = pieces[j]
        group = pl.ds(g * zg, zg)
        return remote(
            pass_ref.at[m % 2, c, group], run_ref.at[m, c, group], run_s.at[m, j], run_r.at[m, j],
            "prow", below,
        )

    def rising(m, j):
        c, g = pieces[j]
        group = pl.ds(g * zg, zg)
        return remote(
            pass_ref.at[m % 2, c, group], meet_ref.at[m, c, group], run_s.at[m, j],
            fall_r.at[m, j], "prow", above,
        )

    def final(m, j):
        c, g = pieces[j]
        return low_gat_ref.at[m, c, pl.ds(g * zg, zg), core]

    def back(m, j):
        return remote(
            final(m, j), final(m, j), back_s.at[m, j], back_r.at[m, j], "prow", above
        )

    def fall(m, j):
        return remote(
            final(m, j), final(m, j), fall_s.at[m, j], back_r.at[m, j], "prow", below
        )

    def back_pair(m, j):
        return remote(
            final(m, j), final(m, j), bpair_s.at[m, j], bpair_r.at[m, j], "prow", partner
        )

    def passed(m, j):
        pl.when(over)(running(m, j).wait_send)
        pl.when(under)(rising(m, j).wait_send)

    def reduce(m):
        crossed(m).wait_recv()
        for j, (c, g) in enumerate(pieces):
            if m >= 2:
                passed(m - 2, j)
            pl.when(fed_above)(running(m, j).wait_recv)
            pl.when(fed_below)(rising(m, j).wait_recv)

            def combine(upper_sum, lower_sum, done, c=c, g=g):
                for z in range(g * zg, (g + 1) * zg):
                    flag = jnp.where(chip == z, 1.0, 0.0).astype(F32)
                    value = low_ref[c, m * hb : (m + 1) * hb, :] * flag
                    value = value - (keep_ref[c, z] + got_ref[m, c, z].astype(F32))
                    if upper_sum:
                        value = value + run_ref[m, c, z].astype(F32)
                    if lower_sum:
                        value = value + meet_ref[m, c, z].astype(F32)
                    if done:
                        low_gat_ref[m, c, z, core] = value.astype(BF16)
                    else:
                        pass_ref[m % 2, c, z] = value.astype(BF16)

            starts = jnp.logical_or(under, both(over, jnp.logical_not(has_above)))
            pl.when(starts)(functools.partial(combine, False, False, False))
            pl.when(both(over, has_above))(functools.partial(combine, True, False, False))
            pl.when(at_root)(functools.partial(combine, root < chips - 1, root > 0, True))
            pl.when(over)(running(m, j).start)
            pl.when(under)(rising(m, j).start)
            begin(both(at_root, feeds[c]), back(m, j))
            begin(both(at_root, has_below), fall(m, j))
            begin(both(at_root, needs[c]), back_pair(m, j))

    def come_back(m, when):
        for j, (c, g) in enumerate(pieces):
            cond = both(both(jnp.logical_not(at_root), needs[c]), when)
            pl.when(cond)(back(m, j).wait_recv)
            begin(both(both(cond, over), feeds[c]), back(m, j))
            begin(cond, back_pair(m, j))

    def lower(m):
        for j, (c, g) in enumerate(pieces):
            pl.when(needs[c])(back_pair(m, j).wait_recv)
        multiply(1, m)

    def ask(step):
        source = lax.rem(here + step, line)
        return remote(
            ask_ref.at[source], asked_ref.at[here], ask_s.at[step - 1], ask_r.at[step - 1],
            "prow", source,
        )

    def spots():
        ids = lax.broadcasted_iota(jnp.int32, (share, count), 0)

        @pl.loop(0, line)
        def _(source):
            hit = jnp.where(ids + source * share == code_ref[...], 1.0, 0.0).astype(BF16)
            spot_ref[span(source, share), :] = hit
            digits = lax.dot_general(digit_ref[...], hit, NT, preferred_element_type=F32)
            wanted = digits[0:1] * BASE + digits[1:2]
            ask_ref[source] = jnp.broadcast_to(wanted, (8, share))

        for step in range(1, line):
            begin(None, ask(step))
        asked_ref[here] = ask_ref[here]

    def picks():
        for step in range(1, line):
            ask(step).wait_recv()
        ids = lax.broadcasted_iota(jnp.int32, (2 * depth, share), 0)

        @pl.loop(0, line)
        def _(target):
            wanted = asked_ref[target][0:1].astype(jnp.int32)
            pick_ref[target] = jnp.where(ids == wanted, 1.0, 0.0).astype(BF16)

    def select_upper(m):
        @pl.loop(0, line)
        def _(target):
            sel_ref[m, target] = lax.dot_general(
                full_ref[m, place], pick_ref[target, depth:], NN, preferred_element_type=F32
            ).astype(BF16)

    def move(m, step):
        target = lax.rem(here + step, line)
        return remote(
            sel_ref.at[m, target], take_ref.at[m, :, span(here, share)],
            move_s.at[m, step - 1], move_r.at[m, step - 1], "prow", target,
        )

    def send_rows(m):
        solved = total_of(1, m)

        def chosen(target):
            low = lax.dot_general(
                solved, pick_ref[target, :depth], NN, preferred_element_type=F32
            )
            return (low + sel_ref[m, target].astype(F32)).astype(BF16)

        for step in range(1, line):
            target = lax.rem(here + step, line)
            sel_ref[m, target] = chosen(target)
            begin(None, move(m, step))
        take_ref[m, :, span(here, share)] = chosen(here)

    def put(m):
        for step in range(1, line):
            move(m, step).wait_recv()

        across = tile_of(count)

        @pl.loop(0, count // across)
        def _(step):
            cols = span(step, across)
            value = lax.dot_general(
                take_ref[m], spot_ref[:, cols], NN, preferred_element_type=F32
            ).astype(BF16)
            out_ref[:, m * hb : (m + 1) * hb, cols] = value.reshape(line // size, hb, across)

    gather_start(0)
    for copy in mats:
        copy.start()
    raw(0).start()
    spots()
    lay(0)
    gather(0)
    if chunks > 1:
        gather_start(1)
    for copy in mats:
        copy.wait()

    def valid(m):
        return 0 <= m < chunks

    far = chip > root + 1
    for t in range(chunks + 7):
        if valid(t - 1):
            settle(t - 1)
        if valid(t):
            gathered(t)
            multiply(0, t)
        if t == 0:
            picks()
            lay(1)
        if valid(t - 3):
            come_back(t - 3, far)
        if valid(t - 3):
            lower(t - 3)
        if valid(t - 4):
            send_rows(t - 4)
        if valid(t - 5):
            put(t - 5)
        if valid(t + 1):
            gather(t + 1)
        if valid(t + 2):
            gather_start(t + 2)
        if valid(t - 1):
            couple(t - 1)
        if valid(t - 1):
            select_upper(t - 1)
        if valid(t - 2):
            come_back(t - 2, jnp.logical_not(far))
        if valid(t - 1):
            reduce(t - 1)
    for m in range(max(0, chunks - 2), chunks):
        for index in range(size - 1):
            summed(0, m, index).wait_send()
            summed(1, m, index).wait_send()
        crossed(m).wait_send()
        for j in range(len(pieces)):
            passed(m, j)
    for cond, copy in ends:
        if cond is None:
            copy.wait_send()
        else:
            pl.when(cond)(copy.wait_send)


def pair_of(*shape):
    return [pltpu.SemaphoreType.DMA(shape)] * 2


def body(right_side, inverse_blocks, coupling, pivots):
    rhs_here = right_side.shape[0]
    width = right_side.shape[3]
    depth = inverse_blocks.shape[1] * width
    tiles = inverse_blocks.shape[4]
    line = lax.axis_size("prow")
    size = lax.axis_size("pcol")
    chunks = chunks_of(rhs_here)
    chips = line // CORES
    hb = rhs_here // chunks
    rows = line * hb
    part = rows // size

    coupling_mat = coupling.reshape(depth, tiles, width)
    sides = right_side.reshape(rhs_here, 2 * tiles, width)
    lower_rhs = sides[:, :tiles].transpose(1, 0, 2)
    upper_rhs = sides[:, tiles:].astype(BF16).transpose(1, 0, 2)

    downward = [(p, p - CORES) for p in range(CORES, line)]
    fell = lax.ppermute(upper_rhs, "prow", downward)
    first = inverse_blocks[1].reshape(depth, tiles * width)
    other, _ = lax.optimization_barrier((inverse_blocks, upper_rhs))
    later = other[0].reshape(depth, tiles * width)
    pivot = pivots.reshape(-1)
    count = pivot.shape[0]
    share = count // line
    owner = pivot // width % line
    local = pivot // (width * line) * width + pivot % width
    same = owner[None, :] == lax.broadcasted_iota(jnp.int32, (line, 1), 0)
    before = lax.broadcasted_iota(jnp.int32, (count, count), 0)
    after = lax.broadcasted_iota(jnp.int32, (count, count), 1)
    counted = jnp.dot(
        same.astype(BF16), (before < after).astype(BF16), preferred_element_type=F32
    )
    rank = jnp.sum(jnp.where(same, counted, 0.0), axis=0).astype(jnp.int32)
    code = owner * share + rank
    digit = lax.broadcasted_iota(jnp.int32, (16, 1), 0)
    digits = jnp.where(
        digit == 0, local // BASE, jnp.where(digit == 1, local % BASE, 0)
    ).astype(BF16)

    strip = (tiles, chips, hb, width)
    pieces = tiles * GROUPS
    vmem, anywhere = pl.BlockSpec(memory_space=pltpu.VMEM), pl.BlockSpec(memory_space=pl.ANY)
    permuted = pl.pallas_call(
        functools.partial(window_kernel, size, line, chunks),
        out_shape=jax.ShapeDtypeStruct((line // size, rhs_here, count), BF16),
        in_specs=[anywhere] * 2 + [vmem] + [anywhere] * 3 + [vmem] * 2,
        out_specs=vmem,
        scratch_shapes=[
            pltpu.VMEM((chunks, tiles, chips, CORES, hb, width), BF16),
            pltpu.VMEM((chunks, tiles, chips, CORES, hb, width), BF16),
            pltpu.VMEM((depth, tiles * width), BF16),
            pltpu.VMEM((depth, tiles * width), BF16),
            pltpu.VMEM((depth, tiles * width), BF16),
            pltpu.VMEM((size, part, depth), F32),
            pltpu.VMEM((2, 2, part, depth), F32),
            pltpu.VMEM((2, 2, size, part, depth), BF16),
            pltpu.VMEM((chunks, size - 1, part, depth), BF16),
            pltpu.VMEM((chunks, size - 1, part, depth), BF16),
            pltpu.VMEM((chunks, size, part, depth), BF16),
            pltpu.VMEM(strip, F32),
            pltpu.VMEM((2, *strip), BF16),
            pltpu.VMEM((chunks, *strip), BF16),
            pltpu.VMEM((2, *strip), BF16),
            pltpu.VMEM((chunks, *strip), BF16),
            pltpu.VMEM((chunks, *strip), BF16),
            pltpu.VMEM((line, 2 * depth, share), BF16),
            pltpu.VMEM((count, count), BF16),
            pltpu.VMEM((chunks, line, part, share), BF16),
            pltpu.VMEM((chunks, part, count), BF16),
            pltpu.VMEM((line, 8, share), F32),
            pltpu.VMEM((line, 8, share), F32),
            pltpu.VMEM((depth // 2, tiles, width), BF16),
            pltpu.SemaphoreType.DMA((4,)),
            pltpu.SemaphoreType.DMA((chunks, 2)),
        ]
        + pair_of(chunks, max(1, chips - 2), tiles)
        + pair_of(chunks, chips - 1, tiles)
        + pair_of(chunks, tiles)
        + pair_of(2, chunks, size - 1)
        + pair_of(chunks, size - 1)
        + pair_of(chunks)
        + pair_of(chunks, pieces)
        + pair_of(chunks, pieces)
        + pair_of(chunks, pieces)
        + pair_of(chunks, pieces)
        + pair_of(chunks, line - 1)
        + pair_of(line - 1),
        compiler_params=pltpu.CompilerParams(
            collective_id=0, has_side_effects=True, vmem_limit_bytes=62 * 1024 * 1024
        ),
        name="window",
    )(
        upper_rhs, fell, lower_rhs, later, first, coupling_mat,
        code.reshape(1, count), digits,
    )
    return permuted.reshape(rhs_here * line // size, pivots.shape[0], 1, width)


def solution(mesh):
    in_specs = (
        P("prow", None, "pcol", None),
        P(None, None, "prow", None, None, "pcol", None),
        P(None, "prow", None, None, "pcol", None),
        P(None, "prow", None),
    )
    out_specs = P("pcol", None, "prow", None)
    return jax.shard_map(body, mesh=mesh, in_specs=in_specs, out_specs=out_specs, check_vma=False)
```
